32 devices in a mesh: parts: 2 (over x), chol: 16 (over z, y, core).
Axes of the slice: x: 2, y: 2, z: 4, core: 2. Of those that a mesh axis runs over, the one named last changes fastest.
Arguments:
- orbitals: float32 [32, 100, 1024], P(('parts', 'chol')), parts along dimension 0, may hold values from -6 to 6
- intersection_inv: float32 [32, 100, 100], P(('parts', 'chol')), parts along dimension 0, may hold values from -0.625 to 0.625
- factor_rows: bfloat16 [4096, 1024], P('chol'), may hold values from -0.1875 to 0.1875
- factor_rotated: bfloat16 [100, 4096], replicated, may hold values from -0.625 to 0.625
- factor_core: bfloat16 [1024, 4096], P('chol'), may hold values from -0.125 to 0.125
- fields: float32 [32, 1024], P('parts', 'chol'), parts along dimension 0, may hold values from -6 to 6
Outputs:
- propagated: float32 [32, 100, 1024], P(('parts', 'chol')), parts along dimension 0
- force_bias: float32 [32, 1024], P('parts', 'chol'), parts along dimension 0
The draws below stay inside these ranges and needn't reach their ends.
There are 2 independent parts, one for each index of `parts`. The reference program is written for one: setup_inputs(seed, part) draws one part's arguments, and reference() takes and returns one part's arrays. A program takes and returns all parts, laid end to end along the dimension named above; an argument that names none is the same for every part. Nothing has to cross between parts.
All inputs are finite; a program needn't handle non-finite values.
Results may differ from the reference program's by a relative error of at most 0.0091.
Values may be sent and summed in bfloat16 or wider, within the bound.
A program may use at most 64 MiB of HBM per device.

```python
import jax
import jax.numpy as jnp
from jax import lax

M = 1024
NE = 100
NP = 4096
TAYLOR = 4
NCHOL = 1024
W = 16


def shard_levels(stream_key, dims, cuts, low, high):
    factor_of = 1.0
    for dim, blocks in cuts:
        draws = jax.random.uniform(jax.random.fold_in(jax.random.fold_in(stream_key, 6), dim), (blocks,), jnp.float32, low / len(cuts), high / len(cuts))
        factor_of = factor_of * jnp.repeat(jnp.exp(draws), dims[dim] // blocks).reshape((-1,) + (1,) * (len(dims) - 1 - dim))
    return factor_of


def normal_values(rng, dims, deviation, most, shards=(), held_as=jnp.bfloat16):
    level = shard_levels(rng, dims, shards, -0.22, 0.18) if shards else 1.0
    entries = jax.random.normal(rng, dims, jnp.float32) * deviation * level
    return jnp.minimum(jnp.maximum(entries, -most), most).astype(held_as)


def setup_inputs(seed: int = 0, part: int = 0) -> dict:
    keys = jax.random.split(jax.random.key(seed), 7)
    own_keys = jax.random.split(jax.random.fold_in(keys[6], part), 7)
    return {
        "orbitals": normal_values(own_keys[0], (W, NE, M), 1.0, 6.0, ((0, 16),), jnp.float32),
        "intersection_inv": normal_values(own_keys[1], (W, NE, NE), NE ** -0.5, 0.625, ((0, 16),), jnp.float32),
        "factor_rows": normal_values(keys[2], (NP, M), M ** -0.5, 0.1875, ((0, 16),)),
        "factor_rotated": normal_values(keys[3], (NE, NP), NE ** -0.5, 0.625),
        "factor_core": normal_values(keys[4], (NCHOL, NP), (NP * NCHOL // (2 * M)) ** -0.5, 0.125, ((0, 16),)),
        "fields": normal_values(own_keys[5], (W, NCHOL), 1.0, 6.0, ((1, 16),), jnp.float32),
    }


def density_one(half_green, factor_rows, factor_rotated):
    projected = lax.dot_general(half_green, factor_rows, (((1,), (1,)), ((), ())), preferred_element_type=jnp.float32)
    return jnp.sum(factor_rotated.astype(jnp.float32) * projected, axis=0).astype(jnp.bfloat16)


def propagate_one(orbital, potential, factor_rows):
    total = orbital
    term = orbital
    for order in range(1, TAYLOR + 1):
        summed = lax.dot_general(term.astype(jnp.bfloat16), factor_rows, (((1,), (1,)), ((), ())), preferred_element_type=jnp.float32)
        scaled = (summed * potential[None, :] / order).astype(jnp.bfloat16)
        term = jnp.dot(scaled, factor_rows, preferred_element_type=jnp.float32)
        total = total + term
    return total


def reference(orbitals, intersection_inv, factor_rows, factor_rotated, factor_core, fields):
    half_green = jnp.einsum("wij,wjm->wim", intersection_inv, orbitals, precision=lax.Precision.HIGHEST).astype(jnp.bfloat16)
    density = lax.map(lambda item: density_one(item, factor_rows, factor_rotated), half_green)
    force_bias = lax.dot_general(density, factor_core, (((1,), (1,)), ((), ())), preferred_element_type=jnp.float32)
    shifted = (fields - force_bias).astype(jnp.bfloat16)
    potential = jnp.dot(shifted, factor_core, preferred_element_type=jnp.float32)
    propagated = lax.map(lambda pair: propagate_one(pair[0], pair[1], factor_rows), (orbitals, potential))
    return propagated, force_bias
```

```python
import functools

import jax
import jax.numpy as jnp
from jax import lax
from jax.experimental import pallas as pl
from jax.experimental.pallas import tpu as pltpu
from jax.sharding import PartitionSpec as P

TAYLOR = 4
F32, BF16 = jnp.float32, jnp.bfloat16
LAST = (((1,), (1,)), ((), ()))


def kernel(
    n, orb_ref, inv_ref, rows_ref, rot_ref, core_ref, fields_ref, out_ref, fb_ref,
    xbuf, xturn, orb3, lhs, pad, rot, corep, s1, sc, dbuf, dlast, dfull, pbuf, rbuf, pot, tbf, total,
    orb_sem, own_sem, rot_sem, core_sem, ring_send, ring_recv, twin_send, twin_recv, pair_send, pair_recv,
    pass_send, pass_recv, side_send, side_recv, mine_send, mine_recv,
    dens_send, dens_recv, dpair_send, dpair_recv, last_send, last_recv, hello_sem, ready_sem, pot_send, pot_recv,
):
    h = n // 2
    p, m = rows_ref.shape
    ne = orb_ref.shape[0]
    nep = pad.shape[0]
    half = h * p
    side_rows = p * 5 // 256 * 16
    sizes = (side_rows, p - 2 * side_rows)
    here = lax.axis_index("parts")
    starts = (here * side_rows, 2 * side_rows)
    me = lax.axis_index("chol")
    q, c = me // 2, me % 2
    partner = q * 2 + (1 - c)
    r = (1 - q % 2) * (q // 2) + (q % 2) * (h - 1 - q // 2)

    def chip_at(pos):
        pos = (pos + 2 * h) % h
        s = pos // (h // 2)
        return (1 - s) * 2 * pos + s * (2 * (h - 1 - pos) + 1)

    def signal(sem, device):
        pl.semaphore_signal(sem, inc=1, device_id=device, device_id_type=pl.DeviceIdType.MESH)

    barrier = pltpu.get_barrier_semaphore()
    ring = ({"chol": chip_at(r + 1) * 2 + c}, {"chol": chip_at(r - 1) * 2 + c})
    for near in ({"chol": partner}, *ring, {"parts": 1 - here}):
        signal(barrier, near)

    def place(chip, core, first, size):
        return pl.ds(pl.multiple_of(core * half + chip * p + first, 16), size)

    orb_copy = pltpu.make_async_copy(orb_ref, orb3, orb_sem)
    orb_copy.start()
    own_copy = pltpu.make_async_copy(rows_ref, xbuf.at[place(q, c, 0, p)], own_sem)
    own_copy.start()
    rot_copy = pltpu.make_async_copy(rot_ref, rot, rot_sem)
    rot_copy.start()
    core_copies = []
    for s in range(n):
        copy = pltpu.make_async_copy(
            core_ref.at[:, pl.ds(s * p, p)],
            corep.at[:, pl.ds((s % 2) * half + (s // 2) * p, p)],
            core_sem.at[s],
        )
        copy.start()
        core_copies.append(copy)

    pl.semaphore_wait(barrier, 4)
    sent = []

    def remote(src, dst, send, recv, target):
        return pltpu.make_async_remote_copy(
            src_ref=src, dst_ref=dst, send_sem=send, recv_sem=recv,
            device_id={"chol": target}, device_id_type=pl.DeviceIdType.MESH,
        )

    def start(copy):
        copy.start()
        sent.append(copy)

    def rows(way, step, part):
        if step < h // 2:
            return pl.multiple_of(starts[part], 16), sizes[part]
        if part == 1:
            return 2 * side_rows + way * (sizes[1] // 2), sizes[1] // 2
        return pl.multiple_of((way + (1 - 2 * way) * here) * side_rows, 16), side_rows

    def slot(chip, core, way, step, part):
        return xbuf.at[place(chip, core, *rows(way, step, part))]

    def twin(way, step, row):
        view = xbuf.at[place(chip_at(r - (1 - 2 * way) * step), c, row, side_rows)]
        return pltpu.make_async_remote_copy(
            src_ref=view, dst_ref=view, send_sem=twin_send.at[way, step - 1], recv_sem=twin_recv.at[way, step - 1],
            device_id={"parts": 1 - here}, device_id_type=pl.DeviceIdType.MESH,
        )

    def hop(way, step, part):
        sign = 1 - 2 * way
        origin = chip_at(r - sign * (step - 1))
        src = rows_ref.at[pl.ds(*rows(way, step, part))] if step == 1 else slot(origin, c, way, step, part)
        return remote(
            src, slot(origin, c, way, step, part), ring_send.at[way, step - 1, part], ring_recv.at[way, step - 1, part],
            chip_at(r + sign) * 2 + c,
        )

    def arrival(way, step, part):
        sign = 1 - 2 * way
        landed = slot(chip_at(r - sign * step), c, way, step, part)
        return remote(
            landed, landed, ring_send.at[way, step - 1, part], ring_recv.at[way, step - 1, part],
            chip_at(r + sign) * 2 + c,
        )

    def passed(core, way, step, part):
        view = slot(chip_at(r - (1 - 2 * way) * step), core, way, step, part)
        return remote(view, view, pass_send.at[way, step - 1, part], pass_recv.at[way, step - 1, part], partner)

    def aside(core, way, step):
        view = xbuf.at[place(chip_at(r - (1 - 2 * way) * step), core, (1 - here) * side_rows, side_rows)]
        return remote(view, view, side_send.at[way, step - 1], side_recv.at[way, step - 1], partner)

    for part in range(2):
        for way in range(2):
            start(hop(way, 1, part))
    start(remote(rows_ref, xbuf.at[place(q, c, 0, p)], mine_send, mine_recv, partner))
    for near in ring:
        signal(hello_sem.at[0], near)

    pad[...] = jnp.zeros_like(pad)
    orb_copy.wait()
    for j in range(m // 128):
        pad[0:ne, j * 128 : (j + 1) * 128] = orb3[:, j]
    total[...] = pad[...]
    lhs[2] = pad[...].astype(BF16)
    pad[0:ne] = jnp.dot(inv_ref[0], pad[0:ne], preferred_element_type=F32, precision=lax.Precision.HIGHEST)
    lhs[c] = pad[...].astype(BF16)
    start(remote(lhs.at[c], lhs.at[c], pair_send, pair_recv, partner))
    dbuf[c, q] = jnp.zeros(dbuf.shape[2:], BF16)
    own_copy.wait()
    rot_copy.wait()
    for k in range(1, h // 2 - 1):
        pl.semaphore_wait(hello_sem.at[k - 1], 2)
        for near in ring:
            signal(hello_sem.at[k], near)
    remote(lhs.at[1 - c], lhs.at[1 - c], pair_send, pair_recv, partner).wait_recv()

    def turn(where):
        xturn[:, where] = xbuf[where, :].T

    def near_block(chip, last=False):
        where = place(chip, c, 0, p)
        result = lax.dot_general(lhs[...].reshape(3 * nep, m), xbuf[where, :], LAST, preferred_element_type=F32)
        rotated = rot[:, pl.ds(pl.multiple_of((chip * 2 + c) * p, p), p)].astype(F32)
        both = [jnp.sum(rotated * result[w * nep : w * nep + ne], axis=0, keepdims=True) for w in range(2)]
        density = jnp.concatenate(both, axis=0).astype(BF16)
        if last:
            dlast[me] = density
        else:
            dbuf[c, q, :, pl.ds(pl.multiple_of(chip * p, p), p)] = density
        s1[:, pl.ds(pl.multiple_of(c * half + chip * p, p), p)] = result[2 * nep : 3 * nep]

    def far_block(chip):
        where = place(chip, 1 - c, 0, p)
        s1[:, pl.ds(pl.multiple_of((1 - c) * half + chip * p, p), p)] = lax.dot_general(
            lhs[2], xbuf[where, :], LAST, preferred_element_type=F32
        )

    def turns(chip):
        for core in range(2):
            first = pl.multiple_of(core * half + chip * p, p)
            xturn[:, pl.ds(first, p)] = xbuf[pl.ds(first, p), :].T

    def ways(step):
        return range(2 if step < h // 2 - 1 else 1)

    def finish(step):
        for way in ways(step):
            twin(way, step, (1 - here) * side_rows).wait_recv()
            start(aside(c, way, step))
        for way in range(2):
            near_block(chip_at(r - (1 - 2 * way) * step))

    def finish_far(step):
        for way in range(2):
            aside(1 - c, way, step).wait_recv()
            for part in range(2):
                passed(1 - c, way, step, part).wait_recv()
        for way in range(2):
            chip = chip_at(r - (1 - 2 * way) * step)
            far_block(chip)
            turns(chip)

    near_block(q)
    remote(rows_ref, xbuf.at[place(q, 1 - c, 0, p)], mine_send, mine_recv, partner).wait_recv()
    far_block(q)
    turns(q)
    for step in range(1, h // 2):
        for part in range(2):
            for way in (1, 0):
                arrival(way, step, part).wait_recv()
                if step < h // 2 - 1 or (way, part) != (1, 0):
                    start(hop(way, step + 1, part))
                if part == 0:
                    start(twin(way, step, here * side_rows))
                start(passed(c, way, step, part))
        if step == 1:
            pl.semaphore_wait(hello_sem.at[h // 2 - 2], 2)
            signal(ready_sem, {"chol": partner})
        if step == h // 2 - 1:
            twin(1, step, (1 - here) * side_rows).wait_recv()
            start(hop(1, step + 1, 0))
            start(aside(c, 1, step))
        if step > 1:
            finish(step - 1)
            finish_far(step - 1)
    finish(h // 2 - 1)
    pl.semaphore_wait(ready_sem, 1)
    for k in range(1, h):
        target = (q + k) % h * 2 + c
        start(remote(dbuf.at[c, q], dbuf.at[c, q], dens_send.at[k - 1], dens_recv.at[k - 1], target))
    step = h // 2
    for part in range(2):
        for way in (1, 0):
            arrival(way, step, part).wait_recv()
            start(passed(c, way, step, part))
    near_block(chip_at(r - step), True)
    order = sorted(range(1, n), key=lambda k: abs(k - n // 2))
    for k in order:
        start(remote(dlast.at[me], dlast.at[me], last_send.at[k - 1], last_recv.at[k - 1], (me + k) % n))
    for k in range(1, h):
        source = (q + h - k) % h
        view = dbuf.at[c, source]
        remote(view, view, dens_send.at[k - 1], dens_recv.at[k - 1], source * 2 + c).wait_recv()
    start(remote(dbuf.at[c], dbuf.at[c], dpair_send, dpair_recv, partner))
    for copy in core_copies:
        copy.wait()
    finish_far(step - 1)
    remote(dbuf.at[1 - c], dbuf.at[1 - c], dpair_send, dpair_recv, partner).wait_recv()
    for s in range(n):
        dfull[2 * (s // 2) : 2 * (s // 2) + 2, (s % 2) * half : (s % 2 + 1) * half] = dbuf[s % 2, s // 2].astype(F32)
    for way in range(2):
        for part in range(2):
            passed(1 - c, way, step, part).wait_recv()
    far_block(chip_at(r - step))
    turns(chip_at(r - step))
    for k in range(1, n):
        source = (me + n - k) % n
        view = dlast.at[source]
        remote(view, view, last_send.at[k - 1], last_recv.at[k - 1], source).wait_recv()
    for s in range(n):
        chip = s // 2
        pos = chip // 2 if chip % 2 == 0 else h - 1 - chip // 2
        first = (s % 2) * half + chip_at(pos + step) * p
        dfull[2 * chip : 2 * chip + 2, first : first + p] = dlast[s].astype(F32)
    force_bias = lax.dot_general(dfull[...].astype(BF16), corep[...], LAST, preferred_element_type=F32)
    fb_ref[...] = force_bias
    shifted = (fields_ref[...] - force_bias).astype(BF16)
    parts = [
        jnp.dot(shifted, corep[:, side * half : (side + 1) * half], preferred_element_type=F32) for side in range(2)
    ]
    for w in range(n):
        pbuf[w] = jnp.concatenate([part[w : w + 1] for part in parts], axis=0).astype(BF16)
    for k in order:
        target = (me + k) % n
        start(remote(pbuf.at[target], rbuf.at[k - 1], pot_send.at[k - 1], pot_recv.at[k - 1], target))
    summed = pbuf[me].astype(F32)
    for k in range(1, n):
        remote(rbuf.at[k - 1], rbuf.at[k - 1], pot_send.at[k - 1], pot_recv.at[k - 1], partner).wait_recv()
        summed = summed + rbuf[k - 1].astype(F32)
    pot[...] = summed

    wide = 512
    for order in range(1, TAYLOR + 1):
        for j in range(n):
            where = slice(j * p, (j + 1) * p)
            if order == 1:
                result = s1[:, where]
            else:
                result = jnp.dot(tbf[...], xturn[:, where], preferred_element_type=F32)
            scale = pot[j // h : j // h + 1, j % h * p : (j % h + 1) * p] / order
            sc[:, where] = (result * scale).astype(BF16)
        for j in range(m // wide):
            where = slice(j * wide, (j + 1) * wide)
            result = jnp.dot(sc[...], xbuf[:, where], preferred_element_type=F32)
            if order < TAYLOR:
                total[:, where] += result
                tbf[:, where] = result.astype(BF16)
            else:
                for i in range(wide // 128):
                    at = slice(j * wide + i * 128, j * wide + (i + 1) * 128)
                    out_ref[:, j * (wide // 128) + i] = total[0:ne, at] + result[0:ne, i * 128 : (i + 1) * 128]
    for copy in sent:
        copy.wait_send()


def fused(orbitals, intersection_inv, factor_rows, factor_rotated, factor_core, fields, n):
    h = n // 2
    p, m = factor_rows.shape
    ne, points = factor_rotated.shape
    nep = -(-ne // 16) * 16
    half = h * p
    walkers = fields.shape[0]
    vmem = pl.BlockSpec(memory_space=pltpu.VMEM)
    hbm = pl.BlockSpec(memory_space=pl.ANY)
    dma = pltpu.SemaphoreType.DMA
    propagated, force_bias = pl.pallas_call(
        functools.partial(kernel, n),
        out_shape=(
            jax.ShapeDtypeStruct((ne, m // 128, 128), F32),
            jax.ShapeDtypeStruct(fields.shape, F32),
        ),
        in_specs=[hbm, vmem, hbm, hbm, hbm, vmem],
        out_specs=(vmem, vmem),
        scratch_shapes=[
            pltpu.VMEM((points, m), BF16),
            pltpu.VMEM((m, points), BF16),
            pltpu.VMEM((ne, m // 128, 128), F32),
            pltpu.VMEM((3, nep, m), BF16),
            pltpu.VMEM((nep, m), F32),
            pltpu.VMEM((ne, points), BF16),
            pltpu.VMEM(factor_core.shape, BF16),
            pltpu.VMEM((nep, points), F32),
            pltpu.VMEM((nep, points), BF16),
            pltpu.VMEM((2, h, 2, half), BF16),
            pltpu.VMEM((n, 2, p), BF16),
            pltpu.VMEM((walkers, points), F32),
            pltpu.VMEM((n, 2, half), BF16),
            pltpu.VMEM((n - 1, 2, half), BF16),
            pltpu.VMEM((2, half), F32),
            pltpu.VMEM((nep, m), BF16),
            pltpu.VMEM((nep, m), F32),
            dma(()),
            dma(()),
            dma(()),
            dma((n,)),
            dma((2, h // 2, 2)),
            dma((2, h // 2, 2)),
            dma((2, h // 2)),
            dma((2, h // 2)),
            dma(()),
            dma(()),
            dma((2, h // 2, 2)),
            dma((2, h // 2, 2)),
            dma((2, h // 2)),
            dma((2, h // 2)),
            dma(()),
            dma(()),
            dma((h - 1,)),
            dma((h - 1,)),
            dma(()),
            dma(()),
            dma((n - 1,)),
            dma((n - 1,)),
            pltpu.SemaphoreType.REGULAR((h // 2 - 1,)),
            pltpu.SemaphoreType.REGULAR,
            dma((n - 1,)),
            dma((n - 1,)),
        ],
        compiler_params=pltpu.CompilerParams(
            collective_id=0, has_side_effects=True, vmem_limit_bytes=60 * 1024 * 1024
        ),
    )(orbitals.reshape(ne, m // 128, 128), intersection_inv, factor_rows, factor_rotated, factor_core, fields)
    return propagated.reshape(orbitals.shape), force_bias


def density_one(half_green, all_rows, factor_rotated):
    projected = lax.dot_general(half_green, all_rows, LAST, preferred_element_type=F32)
    return jnp.sum(factor_rotated.astype(F32) * projected, axis=0).astype(BF16)


def propagate_one(orbital, potential, all_rows):
    total = orbital
    term = orbital
    for order in range(1, TAYLOR + 1):
        summed = lax.dot_general(term.astype(BF16), all_rows, LAST, preferred_element_type=F32)
        scaled = (summed * potential[None, :] / order).astype(BF16)
        term = jnp.dot(scaled, all_rows, preferred_element_type=F32)
        total = total + term
    return total


def plain(orbitals, intersection_inv, factor_rows, factor_rotated, factor_core, fields):
    walker_count = orbitals.shape[0]
    half_green = jnp.einsum(
        "wij,wjm->wim", intersection_inv, orbitals, precision=lax.Precision.HIGHEST
    ).astype(BF16)
    all_rows = lax.all_gather(factor_rows, "chol", axis=0, tiled=True)
    own_density = lax.map(lambda item: density_one(item, all_rows, factor_rotated), half_green)
    density = lax.all_gather(own_density, "chol", axis=0, tiled=True)
    force_bias = lax.dot_general(density, factor_core, LAST, preferred_element_type=F32)
    shifted = (fields - force_bias).astype(BF16)
    partial_sum = jnp.dot(shifted, factor_core, preferred_element_type=F32)
    summed_all = lax.psum(partial_sum, "chol")
    potential = lax.dynamic_slice_in_dim(
        summed_all, lax.axis_index("chol") * walker_count, walker_count, 0
    )
    propagated = lax.map(lambda pair: propagate_one(pair[0], pair[1], all_rows), (orbitals, potential))
    return (propagated, force_bias)


def solution(mesh):
    n = mesh.shape["chol"]

    def on_device(orbitals, intersection_inv, factor_rows, factor_rotated, factor_core, fields):
        args = (orbitals, intersection_inv, factor_rows, factor_rotated, factor_core, fields)
        rows, m = factor_rows.shape
        if orbitals.shape[0] == 1 and n % 4 == 0 and n > 8 and rows % 256 == 0 and mesh.shape["parts"] == 2 and m % 256 == 0:
            return fused(*args, n)
        return plain(*args)

    in_specs = (
        P(("parts", "chol"), None, None),
        P(("parts", "chol"), None, None),
        P("chol", None),
        P(),
        P("chol", None),
        P("parts", "chol"),
    )
    out_specs = (P(("parts", "chol"), None, None), P("parts", "chol"))
    return jax.shard_map(
        on_device, mesh=mesh, in_specs=in_specs, out_specs=out_specs, check_vma=False
    )
```

```python
import functools

import jax
import jax.numpy as jnp
from jax import lax
from jax.experimental import pallas as pl
from jax.experimental.pallas import tpu as pltpu
from jax.sharding import PartitionSpec as P

TAYLOR = 4
F32, BF16 = jnp.float32, jnp.bfloat16
LAST = (((1,), (1,)), ((), ()))


def kernel(
    n, orb_ref, inv_ref, rows_ref, rot_ref, core_ref, fields_ref, out_ref, fb_ref,
    xbuf, xturn, orb3, inv, fields, lhs, pad, rot, corep, s1, sc, dbuf, dlate, dfull, pbuf, rbuf, pot, tbf, total, early,
    orb_sem, inv_sem, fields_sem, own_sem, rot_sem, core_sem, send_sem, ring_recv, twin_recv, pair_recv,
    pass_recv, mine_recv, dens_recv, dpair_recv, late_recv, hello_sem, ready_sem, pot_send, pot_recv,
):
    h = n // 2
    p, m = rows_ref.shape
    ne = orb_ref.shape[0]
    nep = pad.shape[0]
    half = h * p
    side_rows = p * 5 // 256 * 16
    ahead = p // 128 * 16
    offsets, sizes = (0, ahead), (ahead, side_rows - ahead, p - 2 * side_rows)
    here = lax.axis_index("parts")
    me = lax.axis_index("chol")
    q, c = me // 2, me % 2
    partner = q * 2 + (1 - c)
    r = (1 - q % 2) * (q // 2) + (q % 2) * (h - 1 - q // 2)

    def chip_at(pos):
        pos = (pos + 2 * h) % h
        s = pos // (h // 2)
        return (1 - s) * 2 * pos + s * (2 * (h - 1 - pos) + 1)

    def signal(sem, device):
        pl.semaphore_signal(sem, inc=1, device_id=device, device_id_type=pl.DeviceIdType.MESH)

    barrier = pltpu.get_barrier_semaphore()
    ring = ({"chol": chip_at(r + 1) * 2 + c}, {"chol": chip_at(r - 1) * 2 + c})
    for near in ({"chol": partner}, *ring, {"parts": 1 - here}):
        signal(barrier, near)

    def place(chip, core, first, size):
        return pl.ds(pl.multiple_of(core * half + chip * p + first, 16), size)

    own_copy = pltpu.make_async_copy(rows_ref, xbuf.at[place(q, c, 0, p)], own_sem)
    own_copy.start()
    orb_copy = pltpu.make_async_copy(orb_ref, orb3, orb_sem)
    orb_copy.start()
    inv_copy = pltpu.make_async_copy(inv_ref, inv, inv_sem)
    inv_copy.start()
    fields_copy = pltpu.make_async_copy(fields_ref, fields, fields_sem)
    fields_copy.start()
    pl.semaphore_wait(barrier, 4)
    sent = []

    def remote(view, recv, target, dst=None, send=send_sem):
        return pltpu.make_async_remote_copy(
            src_ref=view, dst_ref=view if dst is None else dst, send_sem=send, recv_sem=recv,
            device_id={"chol": target}, device_id_type=pl.DeviceIdType.MESH,
        )

    def arrived(view, recv):
        remote(view, recv, partner).wait_recv()

    def start(copy):
        copy.start()
        sent.append(copy)

    def rows(way, step, part):
        if part < 2:
            side = here if step < h // 2 else way + (1 - 2 * way) * here
            return pl.multiple_of(side * side_rows + offsets[part], 16), sizes[part]
        if step < h // 2:
            return 2 * side_rows, sizes[2]
        return 2 * side_rows + way * (sizes[2] // 2), sizes[2] // 2

    def slot(chip, core, way, step, part):
        return xbuf.at[place(chip, core, *rows(way, step, part))]

    def twin(way, step, part, side):
        row = side * side_rows + offsets[part]
        view = xbuf.at[place(chip_at(r - (1 - 2 * way) * step), c, row, sizes[part])]
        return pltpu.make_async_remote_copy(
            src_ref=view, dst_ref=view,
            send_sem=send_sem, recv_sem=twin_recv.at[way, step - 1, part],
            device_id={"parts": 1 - here}, device_id_type=pl.DeviceIdType.MESH,
        )

    def hop(way, step, part):
        sign = 1 - 2 * way
        view = slot(chip_at(r - sign * (step - 1)), c, way, step, part)
        return remote(view, ring_recv.at[way, step - 1, part], chip_at(r + sign) * 2 + c)

    def arrival(way, step, part):
        arrived(slot(chip_at(r - (1 - 2 * way) * step), c, way, step, part), ring_recv.at[way, step - 1, part])

    def pass_sem(way, step):
        return pass_recv.at[0 if step == h // 2 else way, step - 1]

    def passed(way, step, part):
        return remote(slot(chip_at(r - (1 - 2 * way) * step), c, way, step, part), pass_sem(way, step), partner)

    def aside(way, step, part):
        row = (1 - here) * side_rows + offsets[part]
        view = xbuf.at[place(chip_at(r - (1 - 2 * way) * step), c, row, sizes[part])]
        return remote(view, pass_sem(way, step), partner)

    def passed_block(way, step):
        arrived(xbuf.at[place(chip_at(r - (1 - 2 * way) * step), 1 - c, 0, p)], pass_sem(way, step))

    def across(way, step, part):
        twin(way, step, part, 1 - here).wait_recv()
        start(aside(way, step, part))

    def mine(core):
        return remote(xbuf.at[place(q, core, 0, p)], mine_recv, partner)

    own_copy.wait()
    for part in range(3):
        for way in range(2):
            start(hop(way, 1, part))
    start(mine(c))
    rot_copy = pltpu.make_async_copy(rot_ref, rot, rot_sem)
    rot_copy.start()
    for s in range(n):
        copy = pltpu.make_async_copy(
            core_ref.at[:, pl.ds(s * p, p)],
            corep.at[:, pl.ds((s % 2) * half + (s // 2) * p, p)],
            core_sem,
        )
        copy.start()
    for near in ring:
        signal(hello_sem.at[0], near)

    pad[...] = jnp.zeros_like(pad)
    orb_copy.wait()
    for j in range(m // 128):
        pad[0:ne, j * 128 : (j + 1) * 128] = orb3[:, j]
    total[...] = pad[...]
    lhs[2] = pad[...].astype(BF16)
    inv_copy.wait()
    pad[0:ne] = jnp.dot(inv[:, 0], pad[0:ne], preferred_element_type=F32, precision=lax.Precision.HIGHEST)
    lhs[c] = pad[...].astype(BF16)
    start(remote(lhs.at[c], pair_recv, partner))
    dbuf[c, q] = jnp.zeros(dbuf.shape[2:], BF16)
    rot_copy.wait()
    for k in range(1, h // 2 - 1):
        pl.semaphore_wait(hello_sem.at[k - 1], 2)
        for near in ring:
            signal(hello_sem.at[k], near)
    arrived(lhs.at[1 - c], pair_recv)

    def near_block(chip, late=None):
        where = place(chip, c, 0, p)
        result = lax.dot_general(lhs[...].reshape(3 * nep, m), xbuf[where, :], LAST, preferred_element_type=F32)
        rotated = rot[:, pl.ds(pl.multiple_of((chip * 2 + c) * p, p), p)].astype(F32)
        both = [jnp.sum(rotated * result[w * nep : w * nep + ne], axis=0, keepdims=True) for w in range(2)]
        density = jnp.concatenate(both, axis=0).astype(BF16)
        if late is None:
            dbuf[c, q, :, pl.ds(pl.multiple_of(chip * p, p), p)] = density
        else:
            dlate[me, :, late * p : (late + 1) * p] = density
        s1[:, pl.ds(pl.multiple_of(c * half + chip * p, p), p)] = result[2 * nep : 3 * nep]

    def far_block(chip):
        where = place(chip, 1 - c, 0, p)
        s1[:, pl.ds(pl.multiple_of((1 - c) * half + chip * p, p), p)] = lax.dot_general(
            lhs[2], xbuf[where, :], LAST, preferred_element_type=F32
        )

    def turns(chip):
        for core in range(2):
            first = pl.multiple_of(core * half + chip * p, p)
            xturn[:, pl.ds(first, p)] = xbuf[pl.ds(first, p), :].T

    def near_blocks(step, late=None):
        for way in range(2):
            near_block(chip_at(r - (1 - 2 * way) * step), None if late is None else late + way)

    def finish_far(step):
        for way in range(2):
            passed_block(way, step)
        for way in range(2):
            chip = chip_at(r - (1 - 2 * way) * step)
            far_block(chip)
            turns(chip)

    near_block(q)
    mine(1 - c).wait_recv()
    far_block(q)
    turns(q)
    order = range(n - 1, 0, -1)

    def peer(k):
        flips = [bit for bit in range(k.bit_length()) if k >> bit & 1]
        return me + sum((1 - 2 * (me // 2**bit % 2)) * 2**bit for bit in flips)

    spans = (pl.ds(0, 2 * p), pl.ds(2 * p, p))

    def gather_late(group):
        arrived(dlate.at[pl.ds(0, n - 1), :, spans[group]], late_recv.at[group])
        for s in range(n):
            chip = s // 2
            pos = chip // 2 if chip % 2 == 0 else h - 1 - chip // 2
            for i in ((0, 1), (2,))[group]:
                other = chip_at(pos + ((1 - h // 2), (h // 2 - 1), h // 2)[i])
                first = (s % 2) * half + other * p
                dfull[2 * chip : 2 * chip + 2, first : first + p] = dlate[s, :, i * p : (i + 1) * p].astype(F32)

    final = h // 2 - 1
    for step in range(1, h // 2):
        for part in range(3):
            for way in (1, 0):
                arrival(way, step, part)
                if step < final or way == 0 or part == 2:
                    start(hop(way, step + 1, part))
                if part < 2:
                    start(twin(way, step, part, here))
                start(passed(way, step, part))
            if part == 1 and step > 1:
                for piece in range(2):
                    for way in (1, 0):
                        across(way, step - 1, piece)
                near_blocks(step - 1)
                if step == final:
                    for k in range(1, h):
                        start(remote(dbuf.at[c, q], dens_recv, (q + k) % h * 2 + c))
                    across(1, step, 0)
                    start(hop(1, step + 1, 0))
        if step == final:
            across(1, step, 1)
            start(hop(1, step + 1, 1))
        if step == 1:
            pl.semaphore_wait(hello_sem.at[h // 2 - 2], 2)
            signal(ready_sem, {"chol": partner})
        else:
            finish_far(step - 1)
    for part in range(2):
        across(0, final, part)
    near_blocks(final, 0)
    pl.semaphore_wait(ready_sem, 1)
    for k in order:
        start(remote(dlate.at[me, :, spans[0]], late_recv.at[0], peer(k)))
    step = h // 2
    for turn in range(3):
        for way in (1, 0):
            part = (turn + 2 * way) % 3
            arrival(way, step, part)
            start(passed(way, step, part))
    near_block(chip_at(r - step), 2)
    for k in order:
        start(remote(dlate.at[me, :, spans[1]], late_recv.at[1], peer(k)))
    arrived(dbuf.at[c, pl.ds(0, h - 1)], dens_recv)
    start(remote(dbuf.at[c], dpair_recv, partner))
    fields_copy.wait()
    pltpu.make_async_copy(core_ref, corep, core_sem).wait()
    arrived(dbuf.at[1 - c], dpair_recv)
    for s in range(n):
        dfull[2 * (s // 2) : 2 * (s // 2) + 2, (s % 2) * half : (s % 2 + 1) * half] = dbuf[s % 2, s // 2].astype(F32)
    gather_late(0)
    gather_late(1)
    force_bias = lax.dot_general(dfull[...].astype(BF16), corep[...], LAST, preferred_element_type=F32)
    fb_ref[...] = force_bias
    shifted = (fields[...] - force_bias).astype(BF16)
    run = half // 2
    potentials = []
    for a in range(2):
        parts = [
            jnp.dot(shifted, corep[:, first : first + run], preferred_element_type=F32)
            for first in (a * run, half + a * run)
        ]
        for w in range(n):
            pbuf[a, w] = jnp.concatenate([part[w : w + 1] for part in parts], axis=0).astype(BF16)
        for k in order:
            target = peer(k)
            copy = remote(pbuf.at[a, target], pot_recv.at[a], target, rbuf.at[a, k - 1], pot_send)
            copy.start()
            potentials.append(copy)

    finish_far(final)
    passed_block(0, step)
    far_block(chip_at(r - step))
    turns(chip_at(r - step))
    for copy in sent:
        copy.wait_send()

    wide = 512
    for a in range(2):
        summed = pbuf[a, me].astype(F32)
        arrived(rbuf.at[a], pot_recv.at[a])
        for k in order:
            summed = summed + rbuf[a, k - 1].astype(F32)
        pot[:, a * run : (a + 1) * run] = summed
        for side in range(2):
            where = slice(side * half + a * run, side * half + (a + 1) * run)
            sc[:, where] = (s1[:, where] * summed[side : side + 1]).astype(BF16)
        for j in range(m // wide):
            where = slice(j * wide, (j + 1) * wide)
            result = sum(
                jnp.dot(sc[:, first : first + run], xbuf[first : first + run, where], preferred_element_type=F32)
                for first in (a * run, half + a * run)
            )
            if a == 0:
                early[:, where] = result
            else:
                result = early[:, where] + result
                total[:, where] += result
                tbf[:, where] = result.astype(BF16)
    for order in range(2, TAYLOR + 1):
        for j in range(n):
            where = slice(j * p, (j + 1) * p)
            result = jnp.dot(tbf[...], xturn[:, where], preferred_element_type=F32)
            scale = pot[j // h : j // h + 1, j % h * p : (j % h + 1) * p] / order
            sc[:, where] = (result * scale).astype(BF16)
        for j in range(m // wide):
            where = slice(j * wide, (j + 1) * wide)
            result = jnp.dot(sc[...], xbuf[:, where], preferred_element_type=F32)
            if order < TAYLOR:
                total[:, where] += result
                tbf[:, where] = result.astype(BF16)
            else:
                for i in range(wide // 128):
                    at = slice(j * wide + i * 128, j * wide + (i + 1) * 128)
                    out_ref[:, j * (wide // 128) + i] = total[0:ne, at] + result[0:ne, i * 128 : (i + 1) * 128]
    for copy in potentials:
        copy.wait_send()


def fused(orbitals, intersection_inv, factor_rows, factor_rotated, factor_core, fields, n):
    h = n // 2
    p, m = factor_rows.shape
    ne, points = factor_rotated.shape
    nep = -(-ne // 16) * 16
    half = h * p
    walkers = fields.shape[0]
    vmem = pl.BlockSpec(memory_space=pltpu.VMEM)
    hbm = pl.BlockSpec(memory_space=pl.ANY)
    dma = pltpu.SemaphoreType.DMA
    propagated, force_bias = pl.pallas_call(
        functools.partial(kernel, n),
        out_shape=(pltpu.VMEM((ne, m // 128, 128), F32), pltpu.VMEM(fields.shape, F32)),
        in_specs=[hbm] * 6,
        out_specs=(vmem, vmem),
        scratch_shapes=[
            pltpu.VMEM((points, m), BF16),
            pltpu.VMEM((m, points), BF16),
            pltpu.VMEM((ne, m // 128, 128), F32),
            pltpu.VMEM((ne, 1, ne), F32),
            pltpu.VMEM(fields.shape, F32),
            pltpu.VMEM((3, nep, m), BF16),
            pltpu.VMEM((nep, m), F32),
            pltpu.VMEM((ne, points), BF16),
            pltpu.VMEM(factor_core.shape, BF16),
            pltpu.VMEM((nep, points), F32),
            pltpu.VMEM((nep, points), BF16),
            pltpu.VMEM((2, h, 2, half), BF16),
            pltpu.VMEM((n, 2, 3 * p), BF16),
            pltpu.VMEM((walkers, points), F32),
            pltpu.VMEM((2, n, 2, half // 2), BF16),
            pltpu.VMEM((2, n - 1, 2, half // 2), BF16),
            pltpu.VMEM((2, half), F32),
            pltpu.VMEM((nep, m), BF16),
            pltpu.VMEM((nep, m), F32),
            pltpu.VMEM((nep, m), F32),
            *[dma(())] * 7,
            dma((2, h // 2, 3)),
            dma((2, h // 2 - 1, 2)),
            dma(()),
            dma((2, h // 2)),
            *[dma(())] * 3,
            dma((2,)),
            pltpu.SemaphoreType.REGULAR((h // 2 - 1,)),
            pltpu.SemaphoreType.REGULAR,
            dma(()),
            dma((2,)),
        ],
        compiler_params=pltpu.CompilerParams(
            collective_id=0, has_side_effects=True, vmem_limit_bytes=60 * 1024 * 1024
        ),
    )(orbitals.reshape(ne, m // 128, 128), intersection_inv.reshape(ne, 1, ne), factor_rows, factor_rotated, factor_core, fields)
    pieces = 4
    propagated, force_bias = pl.pallas_call(
        functools.partial(write_out, pieces),
        out_shape=(
            jax.ShapeDtypeStruct(propagated.shape, F32),
            jax.ShapeDtypeStruct(fields.shape, F32),
        ),
        in_specs=[vmem] * 2,
        out_specs=(hbm, hbm),
        scratch_shapes=[dma((pieces + 1,))],
    )(*(pltpu.with_memory_space_constraint(value, pltpu.VMEM) for value in (propagated, force_bias)))
    return propagated.reshape(orbitals.shape), force_bias


def write_out(pieces, propagated, force_bias, out_ref, fb_ref, sem):
    size = propagated.shape[0] // pieces
    copies = [pltpu.make_async_copy(force_bias, fb_ref, sem.at[pieces])]
    for i in range(pieces):
        where = pl.ds(i * size, size)
        copies.append(pltpu.make_async_copy(propagated.at[where], out_ref.at[where], sem.at[i]))
    for copy in copies:
        copy.start()
    for copy in copies:
        copy.wait()


def density_one(half_green, all_rows, factor_rotated):
    projected = lax.dot_general(half_green, all_rows, LAST, preferred_element_type=F32)
    return jnp.sum(factor_rotated.astype(F32) * projected, axis=0).astype(BF16)


def propagate_one(orbital, potential, all_rows):
    total = orbital
    term = orbital
    for order in range(1, TAYLOR + 1):
        summed = lax.dot_general(term.astype(BF16), all_rows, LAST, preferred_element_type=F32)
        scaled = (summed * potential[None, :] / order).astype(BF16)
        term = jnp.dot(scaled, all_rows, preferred_element_type=F32)
        total = total + term
    return total


def plain(orbitals, intersection_inv, factor_rows, factor_rotated, factor_core, fields):
    walker_count = orbitals.shape[0]
    half_green = jnp.einsum(
        "wij,wjm->wim", intersection_inv, orbitals, precision=lax.Precision.HIGHEST
    ).astype(BF16)
    all_rows = lax.all_gather(factor_rows, "chol", axis=0, tiled=True)
    own_density = lax.map(lambda item: density_one(item, all_rows, factor_rotated), half_green)
    density = lax.all_gather(own_density, "chol", axis=0, tiled=True)
    force_bias = lax.dot_general(density, factor_core, LAST, preferred_element_type=F32)
    shifted = (fields - force_bias).astype(BF16)
    partial_sum = jnp.dot(shifted, factor_core, preferred_element_type=F32)
    summed_all = lax.psum(partial_sum, "chol")
    potential = lax.dynamic_slice_in_dim(
        summed_all, lax.axis_index("chol") * walker_count, walker_count, 0
    )
    propagated = lax.map(lambda pair: propagate_one(pair[0], pair[1], all_rows), (orbitals, potential))
    return (propagated, force_bias)


def solution(mesh):
    n = mesh.shape["chol"]

    def on_device(orbitals, intersection_inv, factor_rows, factor_rotated, factor_core, fields):
        args = (orbitals, intersection_inv, factor_rows, factor_rotated, factor_core, fields)
        rows, m = factor_rows.shape
        if orbitals.shape[0] == 1 and n & (n - 1) == 0 and n > 8 and rows % 256 == 0 and mesh.shape["parts"] == 2 and m % 256 == 0:
            return fused(*args, n)
        return plain(*args)

    in_specs = (
        P(("parts", "chol"), None, None),
        P(("parts", "chol"), None, None),
        P("chol", None),
        P(),
        P("chol", None),
        P("parts", "chol"),
    )
    out_specs = (P(("parts", "chol"), None, None), P("parts", "chol"))
    return jax.shard_map(
        on_device, mesh=mesh, in_specs=in_specs, out_specs=out_specs, check_vma=False
    )
```

```python
import functools

import jax
import jax.numpy as jnp
from jax import lax
from jax.experimental import pallas as pl
from jax.experimental.pallas import tpu as pltpu
from jax.sharding import PartitionSpec as P

TAYLOR = 4
F32, BF16 = jnp.float32, jnp.bfloat16
LAST = (((1,), (1,)), ((), ()))


def kernel(
    n, orb_ref, inv_ref, rows_ref, rot_ref, core_ref, fields_ref, out_ref, fb_ref,
    xbuf, xturn, orb3, inv, fields, lhs, pad, rot, corep, s1, sc, dbuf, dlate, dfull, fpart, fother, pbuf, rbuf, pot,
    tbf, total, early,
    orb_sem, inv_sem, fields_sem, own_sem, rot_sem, core_sem, send_sem, pair_recv, guest_recv, share_recv, mine_recv,
    dens_recv, dpair_recv, swap_recv, pot_send, ready_sem, ring_recv, twin_recv, pass_recv, late_recv, pot_recv, hello_sem,
):
    h = n // 2
    p, m = rows_ref.shape
    ne = orb_ref.shape[0]
    nep = pad.shape[0]
    hp = p // 2
    run = h * hp
    side = n * hp
    shared = hp // 2
    size = shared // 2
    final = h // 2
    here = lax.axis_index("parts")
    me = lax.axis_index("chol")
    q, c = me // 2, me % 2
    partner = q * 2 + (1 - c)
    r = (1 - q % 2) * (q // 2) + (q % 2) * (h - 1 - q // 2)
    halves = (here, 1 - here)

    pieces = ((0, 0), (0, size), (0, 2 * size), (0, 3 * size), (1, 2 * size), (1, 3 * size))

    def chip_at(pos):
        pos = (pos + 2 * h) % h
        s = pos // (h // 2)
        return (1 - s) * 2 * pos + s * (2 * (h - 1 - pos) + 1)

    def signal(sem, device):
        pl.semaphore_signal(sem, inc=1, device_id=device, device_id_type=pl.DeviceIdType.MESH)

    barrier = pltpu.get_barrier_semaphore()
    ring = ({"chol": chip_at(r + 1) * 2 + c}, {"chol": chip_at(r - 1) * 2 + c})
    for near in ({"chol": partner}, *ring, {"parts": 1 - here}):
        signal(barrier, near)

    def place(second, core, chip, first, size):
        return pl.ds(pl.multiple_of(second * side + core * run + chip * hp + first, 16), size)

    def columns(second, core, chip):
        return pl.ds(pl.multiple_of(second * side + core * run + chip * hp, hp), hp)

    for second in range(2):
        pltpu.make_async_copy(
            rows_ref.at[pl.ds(pl.multiple_of(halves[second] * hp, hp), hp)], xbuf.at[place(second, c, q, 0, hp)], own_sem
        ).start()
    orb_copy = pltpu.make_async_copy(orb_ref, orb3, orb_sem)
    orb_copy.start()
    inv_copy = pltpu.make_async_copy(inv_ref, inv, inv_sem)
    inv_copy.start()
    fields_copy = pltpu.make_async_copy(fields_ref, fields, fields_sem)
    fields_copy.start()

    pl.semaphore_wait(barrier, 4)
    sent = []

    def remote(view, recv, target, dst=None, send=send_sem):
        return pltpu.make_async_remote_copy(
            src_ref=view, dst_ref=view if dst is None else dst, send_sem=send, recv_sem=recv,
            device_id=target if isinstance(target, dict) else {"chol": target}, device_id_type=pl.DeviceIdType.MESH,
        )

    def arrived(view, recv):
        remote(view, recv, partner).wait_recv()

    def start(copy):
        copy.start()
        sent.append(copy)

    def from_chip(way, step):
        return chip_at(r - (1 - 2 * way) * step)

    def slot(chip, kind):
        second, first = pieces[kind]
        return xbuf.at[place(second, c, chip, first, size)]

    def hop(way, step, kind):
        return remote(slot(from_chip(way, step - 1), kind), ring_recv.at[way, step - 1, kind], dict(ring[way]))

    def pass_sem(second, way, step):
        return pass_recv.at[second, 0 if step == final else way, step - 1]

    def take(way, step, kind):
        view = slot(from_chip(way, step), kind)
        arrived(view, ring_recv.at[way, step - 1, kind])
        if step + 1 < final or (step + 1 == final and way == kind % 2):
            start(hop(way, step + 1, kind))
        second, first = pieces[kind]
        if kind < 2:
            other = xbuf.at[place(1, c, from_chip(way, step), first, size)]
            start(remote(view, twin_recv.at[0 if step == final else way, step - 1], {"parts": 1 - here}, other))
        start(remote(view, pass_sem(second, way, step), partner))

    def take_both(step, *kinds):
        for kind in kinds:
            for way in (1, 0):
                if step < final or way == kind % 2:
                    take(way, step, kind)

    def across(way, step):
        view = xbuf.at[place(1, c, from_chip(way, step), 0, shared)]
        arrived(view, twin_recv.at[way, step - 1])
        start(remote(view, pass_sem(1, way, step), partner))

    pltpu.make_async_copy(rows_ref, xbuf.at[pl.ds(0, p)], own_sem).wait()
    for kind in range(4):
        for way in range(2):
            start(hop(way, 1, kind))
    for second in range(2):
        start(remote(xbuf.at[place(second, c, q, 0, hp)], mine_recv, partner))
    for chip in range(h):
        first = pl.multiple_of((chip * 2 + c) * p + here * hp, hp)
        pltpu.make_async_copy(rot_ref.at[:, pl.ds(first, hp)], rot.at[:, pl.ds(chip * hp, hp)], rot_sem).start()
    for second in range(2):
        for s in range(n):
            first = pl.multiple_of(s * p + halves[second] * hp, hp)
            pltpu.make_async_copy(
                core_ref.at[:, pl.ds(first, hp)],
                corep.at[:, pl.ds(second * side + (s % 2) * run + (s // 2) * hp, hp)],
                core_sem,
            ).start()
    for near in ring:
        signal(hello_sem.at[0], near)

    pad[...] = jnp.zeros_like(pad)
    orb_copy.wait()
    for j in range(m // 128):
        pad[0:ne, j * 128 : (j + 1) * 128] = orb3[:, j]
    total[...] = pad[...]
    lhs[4] = pad[...].astype(BF16)
    inv_copy.wait()
    pad[0:ne] = jnp.dot(inv[:, 0], pad[0:ne], preferred_element_type=F32, precision=lax.Precision.HIGHEST)
    lhs[c] = pad[...].astype(BF16)
    start(remote(lhs.at[c], guest_recv, {"parts": 1 - here}, lhs.at[2 + c]))
    start(remote(lhs.at[c], pair_recv, partner))
    dbuf[c, q] = jnp.zeros(dbuf.shape[2:], BF16)
    for k in range(1, h // 2 - 1):
        pl.semaphore_wait(hello_sem.at[k - 1], 2)
        for near in ring:
            signal(hello_sem.at[k], near)
    arrived(lhs.at[1 - c], pair_recv)
    pltpu.make_async_copy(rot_ref.at[:, pl.ds(0, run)], rot, rot_sem).wait()

    def turn(second, core, chip):
        xturn[:, columns(second, core, chip)] = xbuf[place(second, core, chip, 0, hp), :].T

    def near_block(chip, late=None):
        result = lax.dot_general(
            lhs[...].reshape(5 * nep, m), xbuf[place(0, c, chip, 0, hp), :], LAST, preferred_element_type=F32
        )
        rotated = rot[:, pl.ds(pl.multiple_of(chip * hp, hp), hp)].astype(F32)
        each = [jnp.sum(rotated * result[w * nep : w * nep + ne], axis=0, keepdims=True) for w in range(4)]
        density = jnp.concatenate(each, axis=0).astype(BF16)
        if late is None:
            dbuf[c, q, :, pl.ds(pl.multiple_of(chip * hp, hp), hp)] = density
        else:
            dlate[me, :, late * hp : (late + 1) * hp] = density
        s1[:, columns(0, c, chip)] = result[4 * nep : 5 * nep]

    def block(second, core, chip):
        s1[:, columns(second, core, chip)] = lax.dot_general(
            lhs[4], xbuf[place(second, core, chip, 0, hp), :], LAST, preferred_element_type=F32
        )
        turn(second, core, chip)

    def ways(step):
        return range(2 if step < final else 1)

    def near_blocks(step, late=None):
        for way in ways(step):
            near_block(from_chip(way, step), None if late is None else late + way)

    def far_blocks(second, step):
        for way in ways(step):
            arrived(xbuf.at[place(second, 1 - c, from_chip(way, step), 0, hp)], pass_sem(second, way, step))
            block(second, 1 - c, from_chip(way, step))

    def turns(step):
        for way in ways(step):
            turn(0, c, from_chip(way, step))

    def second_blocks(step):
        for way in ways(step):
            block(1, c, from_chip(way, step))
        far_blocks(1, step)

    order = range(n - 1, 0, -1)

    def peer(k):
        flips = [bit for bit in range(k.bit_length()) if k >> bit & 1]
        return me + sum((1 - 2 * (me // 2**bit % 2)) * 2**bit for bit in flips)

    spans = (pl.ds(0, 2 * hp), pl.ds(2 * hp, hp))

    def send_late(group):
        for k in order:
            start(remote(dlate.at[me, :, spans[group]], late_recv.at[group], peer(k)))

    def spread_rows(value, chip, where):
        for part in range(2):
            dfull[part * n + 2 * chip : part * n + 2 * chip + 2, where] = value[2 * part : 2 * part + 2].astype(F32)

    def gather_late(group):
        arrived(dlate.at[pl.ds(0, n - 1), :, spans[group]], late_recv.at[group])
        for s in range(n):
            chip = s // 2
            pos = chip // 2 if chip % 2 == 0 else h - 1 - chip // 2
            for i in ((0, 1), (2,))[group]:
                other = chip_at(pos + (1 - final, final - 1, final)[i])
                first = (s % 2) * run + other * hp
                spread_rows(dlate[s, :, i * hp : (i + 1) * hp], chip, slice(first, first + hp))

    block(1, c, q)
    arrived(xbuf.at[pl.ds(0, p)], mine_recv)
    block(0, 1 - c, q)
    block(1, 1 - c, q)
    take_both(1, 0, 1, 2, 3)
    pl.semaphore_wait(hello_sem.at[h // 2 - 2], 2)
    signal(ready_sem, {"chol": partner})
    arrived(lhs.at[2 + c], guest_recv)
    start(remote(lhs.at[2 + c], share_recv, partner))
    arrived(lhs.at[3 - c], share_recv)
    near_block(q)
    turn(0, c, q)
    for step in range(2, final):
        take_both(step, 0, 1)
        near_blocks(step - 1)
        if step == final - 1:
            for k in range(1, h):
                start(remote(dbuf.at[c, q], dens_recv, (q + k) % h * 2 + c))
        take_both(step, 2)
        if step < final - 1:
            far_blocks(0, step - 1)
            turns(step - 1)
        take_both(step, 3)
    for kind in (4, 5):
        for way in range(2):
            start(hop(way, 1, kind))
    near_blocks(final - 1, 0)
    pl.semaphore_wait(ready_sem, 1)
    send_late(0)
    for way in range(2):
        across(way, 1)
    far_blocks(0, final - 2)
    turns(final - 2)
    take_both(final, 0, 1, 2, 3)
    near_blocks(final, 2)
    send_late(1)
    for way in range(2):
        across(way, 2)
    take_both(1, 4)
    far_blocks(0, final - 1)
    turns(final - 1)
    take_both(1, 5)
    arrived(dbuf.at[c, pl.ds(0, h - 1)], dens_recv)
    start(remote(dbuf.at[c], dpair_recv, partner))
    fields_copy.wait()
    pltpu.make_async_copy(core_ref, corep, core_sem).wait()
    second_blocks(1)
    arrived(dbuf.at[1 - c], dpair_recv)
    for s in range(n):
        spread_rows(dbuf[s % 2, s // 2], s // 2, slice((s % 2) * run, (s % 2 + 1) * run))
    gather_late(0)
    take_both(2, 4)
    gather_late(1)
    partial = lax.dot_general(dfull[...].astype(BF16), corep[:, 0:side], LAST, preferred_element_type=F32)
    fpart[...] = partial[n : 2 * n]
    start(remote(fpart, swap_recv, {"parts": 1 - here}, fother))
    take_both(2, 5)
    for step in range(3, final):
        for way in range(2):
            across(way, step)
    arrived(fother, swap_recv)
    force_bias = partial[0:n] + fother[...]
    fb_ref[...] = force_bias
    shifted = (fields[...] - force_bias).astype(BF16)
    potentials = []
    for a in range(2):
        parts = [
            jnp.dot(shifted, corep[:, first : first + run], preferred_element_type=F32)
            for first in (a * side, a * side + run)
        ]
        for w in range(n):
            pbuf[a, w] = jnp.concatenate([part[w : w + 1] for part in parts], axis=0).astype(BF16)
        for k in order:
            target = peer(k)
            copy = remote(pbuf.at[a, target], pot_recv.at[a], target, rbuf.at[a, k - 1], pot_send)
            copy.start()
            potentials.append(copy)
    take_both(3, 4)
    second_blocks(2)
    take_both(3, 5)
    far_blocks(0, final)
    turns(final)
    across(0, final)
    take_both(final, 4, 5)
    second_blocks(3)
    second_blocks(final)
    for copy in sent:
        copy.wait_send()

    wide = 512
    for a in range(2):
        half = slice(a * side, (a + 1) * side)
        summed = pbuf[a, me].astype(F32)
        arrived(rbuf.at[a], pot_recv.at[a])
        for k in order:
            summed = summed + rbuf[a, k - 1].astype(F32)
        pot[a] = summed
        for core in range(2):
            where = slice(a * side + core * run, a * side + (core + 1) * run)
            sc[:, where] = (s1[:, where] * summed[core : core + 1]).astype(BF16)
        for j in range(m // wide):
            where = slice(j * wide, (j + 1) * wide)
            result = jnp.dot(sc[:, half], xbuf[half, where], preferred_element_type=F32)
            if a == 0:
                early[:, where] = result
            else:
                result = early[:, where] + result
                total[:, where] += result
                tbf[:, where] = result.astype(BF16)
    for order in range(2, TAYLOR + 1):
        for j in range(n):
            where = slice(j * p, (j + 1) * p)
            result = jnp.dot(tbf[...], xturn[:, where], preferred_element_type=F32)
            a, core, first = j // h, j % h * 2 // h, j % (h // 2) * p
            scale = pot[a, core : core + 1, first : first + p] / order
            sc[:, where] = (result * scale).astype(BF16)
        for j in range(m // wide):
            where = slice(j * wide, (j + 1) * wide)
            result = jnp.dot(sc[...], xbuf[:, where], preferred_element_type=F32)
            if order < TAYLOR:
                total[:, where] += result
                tbf[:, where] = result.astype(BF16)
            else:
                for i in range(wide // 128):
                    at = slice(j * wide + i * 128, j * wide + (i + 1) * 128)
                    out_ref[:, j * (wide // 128) + i] = total[0:ne, at] + result[0:ne, i * 128 : (i + 1) * 128]
    for copy in potentials:
        copy.wait_send()


def fused(orbitals, intersection_inv, factor_rows, factor_rotated, factor_core, fields, n):
    h = n // 2
    p, m = factor_rows.shape
    ne, points = factor_rotated.shape
    nep = -(-ne // 16) * 16
    hp = p // 2
    run, side = h * hp, n * hp
    vmem = pl.BlockSpec(memory_space=pltpu.VMEM)
    hbm = pl.BlockSpec(memory_space=pl.ANY)
    dma = pltpu.SemaphoreType.DMA
    propagated, force_bias = pl.pallas_call(
        functools.partial(kernel, n),
        out_shape=(pltpu.VMEM((ne, m // 128, 128), F32), pltpu.VMEM(fields.shape, F32)),
        in_specs=[hbm] * 6,
        out_specs=(vmem, vmem),
        scratch_shapes=[
            pltpu.VMEM((points, m), BF16),
            pltpu.VMEM((m, points), BF16),
            pltpu.VMEM((ne, m // 128, 128), F32),
            pltpu.VMEM((ne, 1, ne), F32),
            pltpu.VMEM(fields.shape, F32),
            pltpu.VMEM((5, nep, m), BF16),
            pltpu.VMEM((nep, m), F32),
            pltpu.VMEM((ne, run), BF16),
            pltpu.VMEM(factor_core.shape, BF16),
            pltpu.VMEM((nep, points), F32),
            pltpu.VMEM((nep, points), BF16),
            pltpu.VMEM((2, h, 4, run), BF16),
            pltpu.VMEM((n, 4, 3 * hp), BF16),
            pltpu.VMEM((2 * n, side), F32),
            pltpu.VMEM(fields.shape, F32),
            pltpu.VMEM(fields.shape, F32),
            pltpu.VMEM((2, n, 2, run), BF16),
            pltpu.VMEM((2, n - 1, 2, run), BF16),
            pltpu.VMEM((2, 2, run), F32),
            pltpu.VMEM((nep, m), BF16),
            pltpu.VMEM((nep, m), F32),
            pltpu.VMEM((nep, m), F32),
            *[dma(())] * 15,
            pltpu.SemaphoreType.REGULAR,
            dma((2, h // 2, 6)),
            dma((2, h // 2)),
            dma((2, 2, h // 2)),
            dma((2,)),
            dma((2,)),
            pltpu.SemaphoreType.REGULAR((h // 2 - 1,)),
        ],
        compiler_params=pltpu.CompilerParams(
            collective_id=0, has_side_effects=True, vmem_limit_bytes=60 * 1024 * 1024
        ),
    )(
        orbitals.reshape(ne, m // 128, 128), intersection_inv.reshape(ne, 1, ne),
        factor_rows, factor_rotated, factor_core, fields,
    )
    pieces = 4
    propagated, force_bias = pl.pallas_call(
        functools.partial(write_out, pieces),
        out_shape=(
            jax.ShapeDtypeStruct(propagated.shape, F32),
            jax.ShapeDtypeStruct(fields.shape, F32),
        ),
        in_specs=[vmem] * 2,
        out_specs=(hbm, hbm),
        scratch_shapes=[dma((pieces + 1,))],
    )(*(pltpu.with_memory_space_constraint(value, pltpu.VMEM) for value in (propagated, force_bias)))
    return propagated.reshape(orbitals.shape), force_bias


def write_out(pieces, propagated, force_bias, out_ref, fb_ref, sem):
    size = propagated.shape[0] // pieces
    copies = [pltpu.make_async_copy(force_bias, fb_ref, sem.at[pieces])]
    for i in range(pieces):
        where = pl.ds(i * size, size)
        copies.append(pltpu.make_async_copy(propagated.at[where], out_ref.at[where], sem.at[i]))
    for copy in copies:
        copy.start()
    for copy in copies:
        copy.wait()


def density_one(half_green, all_rows, factor_rotated):
    projected = lax.dot_general(half_green, all_rows, LAST, preferred_element_type=F32)
    return jnp.sum(factor_rotated.astype(F32) * projected, axis=0).astype(BF16)


def propagate_one(orbital, potential, all_rows):
    total = orbital
    term = orbital
    for order in range(1, TAYLOR + 1):
        summed = lax.dot_general(term.astype(BF16), all_rows, LAST, preferred_element_type=F32)
        scaled = (summed * potential[None, :] / order).astype(BF16)
        term = jnp.dot(scaled, all_rows, preferred_element_type=F32)
        total = total + term
    return total


def plain(orbitals, intersection_inv, factor_rows, factor_rotated, factor_core, fields):
    walker_count = orbitals.shape[0]
    half_green = jnp.einsum(
        "wij,wjm->wim", intersection_inv, orbitals, precision=lax.Precision.HIGHEST
    ).astype(BF16)
    all_rows = lax.all_gather(factor_rows, "chol", axis=0, tiled=True)
    own_density = lax.map(lambda item: density_one(item, all_rows, factor_rotated), half_green)
    density = lax.all_gather(own_density, "chol", axis=0, tiled=True)
    force_bias = lax.dot_general(density, factor_core, LAST, preferred_element_type=F32)
    shifted = (fields - force_bias).astype(BF16)
    partial_sum = jnp.dot(shifted, factor_core, preferred_element_type=F32)
    summed_all = lax.psum(partial_sum, "chol")
    potential = lax.dynamic_slice_in_dim(
        summed_all, lax.axis_index("chol") * walker_count, walker_count, 0
    )
    propagated = lax.map(lambda pair: propagate_one(pair[0], pair[1], all_rows), (orbitals, potential))
    return (propagated, force_bias)


def solution(mesh):
    n = mesh.shape["chol"]

    def on_device(orbitals, intersection_inv, factor_rows, factor_rotated, factor_core, fields):
        args = (orbitals, intersection_inv, factor_rows, factor_rotated, factor_core, fields)
        rows, m = factor_rows.shape
        if orbitals.shape[0] == 1 and n == 16 and rows % 256 == 0 and mesh.shape["parts"] == 2 and m % 512 == 0:
            return fused(*args, n)
        return plain(*args)

    in_specs = (
        P(("parts", "chol"), None, None),
        P(("parts", "chol"), None, None),
        P("chol", None),
        P(),
        P("chol", None),
        P("parts", "chol"),
    )
    out_specs = (P(("parts", "chol"), None, None), P("parts", "chol"))
    return jax.shard_map(
        on_device, mesh=mesh, in_specs=in_specs, out_specs=out_specs, check_vma=False
    )
```

```python
import functools

import jax
import jax.numpy as jnp
from jax import lax
from jax.experimental import pallas as pl
from jax.experimental.pallas import tpu as pltpu
from jax.sharding import PartitionSpec as P

TAYLOR = 4
F32, BF16 = jnp.float32, jnp.bfloat16
LAST = (((1,), (1,)), ((), ()))


def kernel(
    n, orb_ref, inv_ref, rows_ref, rot_ref, core_ref, fields_ref, out_ref, fb_ref,
    xbuf, xturn, orb3, inv, fields, lhs, pad, rot, corep, s1, sc, dbuf, dlast, dguest, dfull, dtail, fpart, fother, pbuf, rbuf, pot,
    tbf, total, early,
    orb_sem, inv_sem, fields_sem, own_sem, rot_sem, core_sem, send_sem, pair_recv, guest_recv, share_recv, mine_recv,
    dens_recv, dpair_recv, swap_recv, pot_send, ready_sem, all_sem, ring_recv, twin_recv, extra_recv, pass_recv, last_recv, pot_recv, hello_sem,
):
    h = n // 2
    p, m = rows_ref.shape
    ne = orb_ref.shape[0]
    nep = pad.shape[0]
    hp = p // 2
    run = h * hp
    side = n * hp
    shared = hp // 2
    size = shared // 2
    final = h // 2
    here = lax.axis_index("parts")
    me = lax.axis_index("chol")
    q, c = me // 2, me % 2
    partner = q * 2 + (1 - c)
    r = (1 - q % 2) * (q // 2) + (q % 2) * (h - 1 - q // 2)
    halves = (here, 1 - here)

    pieces = ((0, 0), (0, size), (0, 2 * size), (0, 3 * size), (1, 2 * size), (1, 3 * size))

    def chip_at(pos):
        pos = (pos + 2 * h) % h
        s = pos // (h // 2)
        return (1 - s) * 2 * pos + s * (2 * (h - 1 - pos) + 1)

    def signal(sem, device):
        pl.semaphore_signal(sem, inc=1, device_id=device, device_id_type=pl.DeviceIdType.MESH)

    barrier = pltpu.get_barrier_semaphore()
    ring = ({"chol": chip_at(r + 1) * 2 + c}, {"chol": chip_at(r - 1) * 2 + c})
    for near in ({"chol": partner}, *ring, {"parts": 1 - here}):
        signal(barrier, near)

    def place(second, core, chip, first, size):
        return pl.ds(pl.multiple_of(second * side + core * run + chip * hp + first, 16), size)

    def columns(second, core, chip):
        return pl.ds(pl.multiple_of(second * side + core * run + chip * hp, hp), hp)

    for second in range(2):
        pltpu.make_async_copy(
            rows_ref.at[pl.ds(pl.multiple_of(halves[second] * hp, hp), hp)], xbuf.at[place(second, c, q, 0, hp)], own_sem
        ).start()
    orb_copy = pltpu.make_async_copy(orb_ref, orb3, orb_sem)
    orb_copy.start()
    inv_copy = pltpu.make_async_copy(inv_ref, inv, inv_sem)
    inv_copy.start()
    fields_copy = pltpu.make_async_copy(fields_ref, fields, fields_sem)
    fields_copy.start()

    pl.semaphore_wait(barrier, 4)
    sent = []

    def remote(view, recv, target, dst=None, send=send_sem):
        return pltpu.make_async_remote_copy(
            src_ref=view, dst_ref=view if dst is None else dst, send_sem=send, recv_sem=recv,
            device_id=target if isinstance(target, dict) else {"chol": target}, device_id_type=pl.DeviceIdType.MESH,
        )

    def arrived(view, recv):
        remote(view, recv, partner).wait_recv()

    def start(copy):
        copy.start()
        sent.append(copy)

    def from_chip(way, step):
        return chip_at(r - (1 - 2 * way) * step)

    def slot(chip, kind):
        second, first = pieces[kind]
        return xbuf.at[place(second, c, chip, first, size)]

    def hop(way, step, kind):
        return remote(slot(from_chip(way, step - 1), kind), ring_recv.at[way, step - 1, kind], dict(ring[way]))

    def pass_sem(second, way, step):
        return pass_recv.at[second, 0 if step == final else way, step - 1]

    def travels(way, step, kind):
        if step < final:
            return (step, kind) != (final - 1, 5)
        return step == final and kind < 4 and way == kind % 2

    def take(way, step, kind):
        view = slot(from_chip(way, step), kind)
        arrived(view, ring_recv.at[way, step - 1, kind])
        if travels(way, step + 1, kind):
            start(hop(way, step + 1, kind))
        if kind < 2 and step < final:
            share(way, step, kind)
        start(remote(view, pass_sem(pieces[kind][0], way, step), partner))

    def share(way, step, kind):
        chip = from_chip(way, step)
        other = xbuf.at[place(1, c, chip, pieces[kind][1], size)]
        if step == final:
            arrives = twin_recv.at[kind // 2, step - 1]
        else:
            arrives = twin_recv.at[way, step - 1] if kind < 2 else extra_recv.at[way]
        start(remote(slot(chip, kind), arrives, {"parts": 1 - here}, other))

    def take_both(step, *kinds):
        for kind in kinds:
            for way in (1, 0):
                if travels(way, step, kind):
                    take(way, step, kind)

    def across(way, step):
        first = way * shared if step == final else 0
        view = xbuf.at[place(1, c, from_chip(way, step), first, shared)]
        arrived(view, twin_recv.at[way, step - 1])
        start(remote(view, pass_sem(1, way, step), partner))

    def across_extra(way):
        view = xbuf.at[place(1, c, from_chip(way, final - 1), 3 * size, size)]
        arrived(view, extra_recv.at[way])
        start(remote(view, pass_sem(1, way, final - 1), partner))

    pltpu.make_async_copy(rows_ref, xbuf.at[pl.ds(0, p)], own_sem).wait()
    for kind in range(4):
        for way in range(2):
            start(hop(way, 1, kind))
    for second in range(2):
        start(remote(xbuf.at[place(second, c, q, 0, hp)], mine_recv, partner))
    for chip in range(h):
        first = pl.multiple_of((chip * 2 + c) * p + here * hp, hp)
        pltpu.make_async_copy(rot_ref.at[:, pl.ds(first, hp)], rot.at[:, pl.ds(chip * hp, hp)], rot_sem).start()
    for second in range(2):
        for s in range(n):
            first = pl.multiple_of(s * p + halves[second] * hp, hp)
            pltpu.make_async_copy(
                core_ref.at[:, pl.ds(first, hp)],
                corep.at[:, pl.ds(second * side + (s % 2) * run + (s // 2) * hp, hp)],
                core_sem,
            ).start()
    for near in ring:
        signal(hello_sem.at[0], near)

    pad[...] = jnp.zeros_like(pad)
    orb_copy.wait()
    for j in range(m // 128):
        pad[0:ne, j * 128 : (j + 1) * 128] = orb3[:, j]
    total[...] = pad[...]
    lhs[4] = pad[...].astype(BF16)
    inv_copy.wait()
    pad[0:ne] = jnp.dot(inv[:, 0], pad[0:ne], preferred_element_type=F32, precision=lax.Precision.HIGHEST)
    lhs[c] = pad[...].astype(BF16)
    start(remote(lhs.at[c], guest_recv, {"parts": 1 - here}, lhs.at[2 + c]))
    start(remote(lhs.at[c], pair_recv, partner))
    dbuf[c, q] = jnp.zeros(dbuf.shape[2:], BF16)
    dtail[...] = jnp.zeros_like(dtail)
    for k in range(1, h // 2 - 1):
        pl.semaphore_wait(hello_sem.at[k - 1], 2)
        for near in ring:
            signal(hello_sem.at[k], near)
    arrived(lhs.at[1 - c], pair_recv)
    pltpu.make_async_copy(rot_ref.at[:, pl.ds(0, run)], rot, rot_sem).wait()

    def turn(second, core, chip):
        xturn[:, columns(second, core, chip)] = xbuf[place(second, core, chip, 0, hp), :].T

    def near_block(chip, last=False):
        result = lax.dot_general(
            lhs[...].reshape(5 * nep, m), xbuf[place(0, c, chip, 0, hp), :], LAST, preferred_element_type=F32
        )
        rotated = rot[:, pl.ds(pl.multiple_of(chip * hp, hp), hp)].astype(F32)
        each = [jnp.sum(rotated * result[w * nep : w * nep + ne], axis=0, keepdims=True) for w in range(4)]
        if last:
            dlast[0, me] = jnp.concatenate(each[:2], axis=0).astype(BF16)
            dguest[...] = jnp.concatenate(each[2:], axis=0).astype(BF16)
        else:
            density = jnp.concatenate(each, axis=0).astype(BF16)
            dbuf[c, q, :, pl.ds(pl.multiple_of(chip * hp, hp), hp)] = density
        s1[:, columns(0, c, chip)] = result[4 * nep : 5 * nep]

    def block(second, core, chip):
        s1[:, columns(second, core, chip)] = lax.dot_general(
            lhs[4], xbuf[place(second, core, chip, 0, hp), :], LAST, preferred_element_type=F32
        )
        turn(second, core, chip)

    def ways(step):
        return range(2 if step < final else 1)

    def near_blocks(step):
        for way in ways(step):
            near_block(from_chip(way, step), step == final)

    def far_blocks(second, step):
        for way in ways(step):
            arrived(xbuf.at[place(second, 1 - c, from_chip(way, step), 0, hp)], pass_sem(second, way, step))
            block(second, 1 - c, from_chip(way, step))

    def turns(step):
        for way in ways(step):
            turn(0, c, from_chip(way, step))

    def second_blocks(step):
        for way in ways(step):
            block(1, c, from_chip(way, step))
        far_blocks(1, step)

    order = range(n - 1, 0, -1)

    def peer(k):
        flips = [bit for bit in range(k.bit_length()) if k >> bit & 1]
        return me + sum((1 - 2 * (me // 2**bit % 2)) * 2**bit for bit in flips)

    def send_last():
        for k in range(n - 1, -1, -1):
            target = peer(k)
            if k:
                start(remote(dlast.at[0, me], last_recv.at[0], target))
            start(remote(dguest, last_recv.at[1], {"parts": 1 - here, "chol": target}, dlast.at[1, me]))

    def gather_last():
        for guest in range(2):
            arrived(dlast.at[guest, pl.ds(0, n - 1 + guest)], last_recv.at[guest])
            for s in range(n):
                chip = s // 2
                pos = chip // 2 if chip % 2 == 0 else h - 1 - chip // 2
                first = guest * side + (s % 2) * run + chip_at(pos + final) * hp
                dtail[2 * chip : 2 * chip + 2, first : first + hp] = dlast[guest, s].astype(F32)

    block(1, c, q)
    arrived(xbuf.at[pl.ds(0, p)], mine_recv)
    block(0, 1 - c, q)
    block(1, 1 - c, q)
    take_both(1, 0, 1, 2, 3)
    pl.semaphore_wait(hello_sem.at[h // 2 - 2], 2)
    signal(ready_sem, {"chol": partner})
    arrived(lhs.at[2 + c], guest_recv)
    start(remote(lhs.at[2 + c], share_recv, partner))
    arrived(lhs.at[3 - c], share_recv)
    near_block(q)
    turn(0, c, q)
    for step in range(2, final):
        take_both(step, 0, 1)
        near_blocks(step - 1)
        take_both(step, 2)
        if step < final - 1:
            far_blocks(0, step - 1)
            turns(step - 1)
        take_both(step, 3)
    near_blocks(final - 1)
    for k in range(1, h):
        start(remote(dbuf.at[c, q], dens_recv, (q + k) % h * 2 + c))
    for kind in (4, 5):
        for way in range(2):
            start(hop(way, 1, kind))
    pl.semaphore_wait(ready_sem, 1)
    signal(all_sem, {"parts": 1 - here})
    for way in range(2):
        across(way, 1)
    far_blocks(0, final - 2)
    turns(final - 2)
    take_both(final, 0, 1, 2, 3)
    near_blocks(final)
    pl.semaphore_wait(all_sem, 1)
    send_last()
    for kind in (0, 1):
        share(0, final, kind)
    for way in range(2):
        across(way, 2)
    take_both(1, 4)
    arrived(dbuf.at[c, pl.ds(0, h - 1)], dens_recv)
    start(remote(dbuf.at[c], dpair_recv, partner))
    far_blocks(0, final - 1)
    turns(final - 1)
    take_both(1, 5)
    fields_copy.wait()
    pltpu.make_async_copy(core_ref, corep, core_sem).wait()
    arrived(dbuf.at[1 - c], dpair_recv)
    for s in range(n):
        for part in range(2):
            rows = slice(part * n + 2 * (s // 2), part * n + 2 * (s // 2) + 2)
            value = dbuf[s % 2, s // 2, 2 * part : 2 * part + 2]
            dfull[rows, (s % 2) * run : (s % 2 + 1) * run] = value.astype(F32)
    partial = lax.dot_general(dfull[...].astype(BF16), corep[:, 0:side], LAST, preferred_element_type=F32)
    fpart[...] = partial[n : 2 * n]
    start(remote(fpart, swap_recv, {"parts": 1 - here}, fother))
    for kind in (2, 3):
        share(0, final, kind)
    for way in range(2):
        share(way, final - 1, 3)
    second_blocks(1)
    take_both(2, 4)
    gather_last()
    last = lax.dot_general(dtail[...].astype(BF16), corep[...], LAST, preferred_element_type=F32)
    take_both(2, 5)
    arrived(fother, swap_recv)
    force_bias = partial[0:n] + fother[...] + last
    fb_ref[...] = force_bias
    shifted = (fields[...] - force_bias).astype(BF16)
    potentials = []
    for a in range(2):
        parts = [
            jnp.dot(shifted, corep[:, first : first + run], preferred_element_type=F32)
            for first in (a * side, a * side + run)
        ]
        for w in range(n):
            pbuf[a, w] = jnp.concatenate([part[w : w + 1] for part in parts], axis=0).astype(BF16)
        for k in order:
            target = peer(k)
            copy = remote(pbuf.at[a, target], pot_recv.at[a], target, rbuf.at[a, k - 1], pot_send)
            copy.start()
            potentials.append(copy)
    for way in range(2):
        across(way, final - 1)
    second_blocks(2)
    far_blocks(0, final)
    turns(final)
    for way in range(2):
        across(way, final)
    take_both(final - 1, 4)
    for way in range(2):
        across_extra(way)
    second_blocks(final)
    second_blocks(final - 1)
    for copy in sent:
        copy.wait_send()

    wide = 512
    for a in range(2):
        half = slice(a * side, (a + 1) * side)
        summed = pbuf[a, me].astype(F32)
        arrived(rbuf.at[a], pot_recv.at[a])
        for k in order:
            summed = summed + rbuf[a, k - 1].astype(F32)
        pot[a] = summed
        for core in range(2):
            where = slice(a * side + core * run, a * side + (core + 1) * run)
            sc[:, where] = (s1[:, where] * summed[core : core + 1]).astype(BF16)
        for j in range(m // wide):
            where = slice(j * wide, (j + 1) * wide)
            result = jnp.dot(sc[:, half], xbuf[half, where], preferred_element_type=F32)
            if a == 0:
                early[:, where] = result
            else:
                result = early[:, where] + result
                total[:, where] += result
                tbf[:, where] = result.astype(BF16)
    for order in range(2, TAYLOR + 1):
        for j in range(n):
            where = slice(j * p, (j + 1) * p)
            result = jnp.dot(tbf[...], xturn[:, where], preferred_element_type=F32)
            a, core, first = j // h, j % h * 2 // h, j % (h // 2) * p
            scale = pot[a, core : core + 1, first : first + p] / order
            sc[:, where] = (result * scale).astype(BF16)
        for j in range(m // wide):
            where = slice(j * wide, (j + 1) * wide)
            result = jnp.dot(sc[...], xbuf[:, where], preferred_element_type=F32)
            if order < TAYLOR:
                total[:, where] += result
                tbf[:, where] = result.astype(BF16)
            else:
                for i in range(wide // 128):
                    at = slice(j * wide + i * 128, j * wide + (i + 1) * 128)
                    out_ref[:, j * (wide // 128) + i] = total[0:ne, at] + result[0:ne, i * 128 : (i + 1) * 128]
    for copy in potentials:
        copy.wait_send()


def fused(orbitals, intersection_inv, factor_rows, factor_rotated, factor_core, fields, n):
    h = n // 2
    p, m = factor_rows.shape
    ne, points = factor_rotated.shape
    nep = -(-ne // 16) * 16
    hp = p // 2
    run, side = h * hp, n * hp
    vmem = pl.BlockSpec(memory_space=pltpu.VMEM)
    hbm = pl.BlockSpec(memory_space=pl.ANY)
    dma = pltpu.SemaphoreType.DMA
    propagated, force_bias = pl.pallas_call(
        functools.partial(kernel, n),
        out_shape=(pltpu.VMEM((ne, m // 128, 128), F32), pltpu.VMEM(fields.shape, F32)),
        in_specs=[hbm] * 6,
        out_specs=(vmem, vmem),
        scratch_shapes=[
            pltpu.VMEM((points, m), BF16),
            pltpu.VMEM((m, points), BF16),
            pltpu.VMEM((ne, m // 128, 128), F32),
            pltpu.VMEM((ne, 1, ne), F32),
            pltpu.VMEM(fields.shape, F32),
            pltpu.VMEM((5, nep, m), BF16),
            pltpu.VMEM((nep, m), F32),
            pltpu.VMEM((ne, run), BF16),
            pltpu.VMEM(factor_core.shape, BF16),
            pltpu.VMEM((nep, points), F32),
            pltpu.VMEM((nep, points), BF16),
            pltpu.VMEM((2, h, 4, run), BF16),
            pltpu.VMEM((2, n, 2, hp), BF16),
            pltpu.VMEM((2, hp), BF16),
            pltpu.VMEM((2 * n, side), F32),
            pltpu.VMEM((n, points), F32),
            pltpu.VMEM(fields.shape, F32),
            pltpu.VMEM(fields.shape, F32),
            pltpu.VMEM((2, n, 2, run), BF16),
            pltpu.VMEM((2, n - 1, 2, run), BF16),
            pltpu.VMEM((2, 2, run), F32),
            pltpu.VMEM((nep, m), BF16),
            pltpu.VMEM((nep, m), F32),
            pltpu.VMEM((nep, m), F32),
            *[dma(())] * 15,
            pltpu.SemaphoreType.REGULAR,
            pltpu.SemaphoreType.REGULAR,
            dma((2, h // 2, 6)),
            dma((2, h // 2)),
            dma((2,)),
            dma((2, 2, h // 2)),
            dma((2,)),
            dma((2,)),
            pltpu.SemaphoreType.REGULAR((h // 2 - 1,)),
        ],
        compiler_params=pltpu.CompilerParams(
            collective_id=0, has_side_effects=True, vmem_limit_bytes=60 * 1024 * 1024
        ),
    )(
        orbitals.reshape(ne, m // 128, 128), intersection_inv.reshape(ne, 1, ne),
        factor_rows, factor_rotated, factor_core, fields,
    )
    pieces = 4
    propagated, force_bias = pl.pallas_call(
        functools.partial(write_out, pieces),
        out_shape=(
            jax.ShapeDtypeStruct(propagated.shape, F32),
            jax.ShapeDtypeStruct(fields.shape, F32),
        ),
        in_specs=[vmem] * 2,
        out_specs=(hbm, hbm),
        scratch_shapes=[dma((pieces + 1,))],
    )(*(pltpu.with_memory_space_constraint(value, pltpu.VMEM) for value in (propagated, force_bias)))
    return propagated.reshape(orbitals.shape), force_bias


def write_out(pieces, propagated, force_bias, out_ref, fb_ref, sem):
    size = propagated.shape[0] // pieces
    copies = [pltpu.make_async_copy(force_bias, fb_ref, sem.at[pieces])]
    for i in range(pieces):
        where = pl.ds(i * size, size)
        copies.append(pltpu.make_async_copy(propagated.at[where], out_ref.at[where], sem.at[i]))
    for copy in copies:
        copy.start()
    for copy in copies:
        copy.wait()


def density_one(half_green, all_rows, factor_rotated):
    projected = lax.dot_general(half_green, all_rows, LAST, preferred_element_type=F32)
    return jnp.sum(factor_rotated.astype(F32) * projected, axis=0).astype(BF16)


def propagate_one(orbital, potential, all_rows):
    total = orbital
    term = orbital
    for order in range(1, TAYLOR + 1):
        summed = lax.dot_general(term.astype(BF16), all_rows, LAST, preferred_element_type=F32)
        scaled = (summed * potential[None, :] / order).astype(BF16)
        term = jnp.dot(scaled, all_rows, preferred_element_type=F32)
        total = total + term
    return total


def plain(orbitals, intersection_inv, factor_rows, factor_rotated, factor_core, fields):
    walker_count = orbitals.shape[0]
    half_green = jnp.einsum(
        "wij,wjm->wim", intersection_inv, orbitals, precision=lax.Precision.HIGHEST
    ).astype(BF16)
    all_rows = lax.all_gather(factor_rows, "chol", axis=0, tiled=True)
    own_density = lax.map(lambda item: density_one(item, all_rows, factor_rotated), half_green)
    density = lax.all_gather(own_density, "chol", axis=0, tiled=True)
    force_bias = lax.dot_general(density, factor_core, LAST, preferred_element_type=F32)
    shifted = (fields - force_bias).astype(BF16)
    partial_sum = jnp.dot(shifted, factor_core, preferred_element_type=F32)
    summed_all = lax.psum(partial_sum, "chol")
    potential = lax.dynamic_slice_in_dim(
        summed_all, lax.axis_index("chol") * walker_count, walker_count, 0
    )
    propagated = lax.map(lambda pair: propagate_one(pair[0], pair[1], all_rows), (orbitals, potential))
    return (propagated, force_bias)


def solution(mesh):
    n = mesh.shape["chol"]

    def on_device(orbitals, intersection_inv, factor_rows, factor_rotated, factor_core, fields):
        args = (orbitals, intersection_inv, factor_rows, factor_rotated, factor_core, fields)
        rows, m = factor_rows.shape
        if orbitals.shape[0] == 1 and n == 16 and rows % 256 == 0 and mesh.shape["parts"] == 2 and m % 512 == 0:
            return fused(*args, n)
        return plain(*args)

    in_specs = (
        P(("parts", "chol"), None, None),
        P(("parts", "chol"), None, None),
        P("chol", None),
        P(),
        P("chol", None),
        P("parts", "chol"),
    )
    out_specs = (P(("parts", "chol"), None, None), P("parts", "chol"))
    return jax.shard_map(
        on_device, mesh=mesh, in_specs=in_specs, out_specs=out_specs, check_vma=False
    )
```

```python
import functools

import jax
import jax.numpy as jnp
from jax import lax
from jax.experimental import pallas as pl
from jax.experimental.pallas import tpu as pltpu
from jax.sharding import PartitionSpec as P

TAYLOR = 4
F32, BF16 = jnp.float32, jnp.bfloat16
LAST = (((1,), (1,)), ((), ()))


def kernel(
    n, orb_ref, inv_ref, rows_ref, rot_ref, core_ref, fields_ref, out_ref, fb_ref,
    xbuf, xturn, orb3, inv, fields, lhs, pad, rot, corep, s1, sc, dbuf, dlast, dguest, dfull, dtail, fpart, fother, pbuf, rbuf, pot,
    tbf, total, early,
    orb_sem, inv_sem, fields_sem, own_sem, rot_sem, core_sem, send_sem, pair_recv, guest_recv, share_recv, mine_recv,
    dens_recv, dpair_recv, swap_recv, pot_send, ready_sem, all_sem, ring_recv, twin_recv, extra_recv, pass_recv, last_recv, pot_recv, hello_sem,
):
    h = n // 2
    p, m = rows_ref.shape
    ne = orb_ref.shape[0]
    nep = pad.shape[0]
    hp = p // 2
    run = h * hp
    side = n * hp
    shared = hp // 2
    size = shared // 2
    final = h // 2
    here = lax.axis_index("parts")
    me = lax.axis_index("chol")
    q, c = me // 2, me % 2
    partner = q * 2 + (1 - c)
    r = (1 - q % 2) * (q // 2) + (q % 2) * (h - 1 - q // 2)
    halves = (here, 1 - here)

    pieces = ((0, 0), (0, size), (0, 2 * size), (0, 3 * size), (1, 2 * size), (1, 3 * size))

    def chip_at(pos):
        pos = (pos + 2 * h) % h
        s = pos // (h // 2)
        return (1 - s) * 2 * pos + s * (2 * (h - 1 - pos) + 1)

    def signal(sem, device):
        pl.semaphore_signal(sem, inc=1, device_id=device, device_id_type=pl.DeviceIdType.MESH)

    barrier = pltpu.get_barrier_semaphore()
    ring = ({"chol": chip_at(r + 1) * 2 + c}, {"chol": chip_at(r - 1) * 2 + c})
    for near in ({"chol": partner}, *ring, {"parts": 1 - here}):
        signal(barrier, near)

    def place(second, core, chip, first, size):
        return pl.ds(pl.multiple_of(second * side + core * run + chip * hp + first, 16), size)

    def columns(second, core, chip):
        return pl.ds(pl.multiple_of(second * side + core * run + chip * hp, hp), hp)

    for second in range(2):
        pltpu.make_async_copy(
            rows_ref.at[pl.ds(pl.multiple_of(halves[second] * hp, hp), hp)], xbuf.at[place(second, c, q, 0, hp)], own_sem
        ).start()
    orb_copy = pltpu.make_async_copy(orb_ref, orb3, orb_sem)
    orb_copy.start()
    inv_copy = pltpu.make_async_copy(inv_ref, inv, inv_sem)
    inv_copy.start()
    fields_copy = pltpu.make_async_copy(fields_ref, fields, fields_sem)
    fields_copy.start()

    pl.semaphore_wait(barrier, 4)
    sent = []

    def remote(view, recv, target, dst=None, send=send_sem):
        return pltpu.make_async_remote_copy(
            src_ref=view, dst_ref=view if dst is None else dst, send_sem=send, recv_sem=recv,
            device_id=target if isinstance(target, dict) else {"chol": target}, device_id_type=pl.DeviceIdType.MESH,
        )

    def arrived(view, recv):
        remote(view, recv, partner).wait_recv()

    def start(copy):
        copy.start()
        sent.append(copy)

    def from_chip(way, step):
        return chip_at(r - (1 - 2 * way) * step)

    def slot(chip, kind):
        second, first = pieces[kind]
        return xbuf.at[place(second, c, chip, first, size)]

    def hop(way, step, kind):
        return remote(slot(from_chip(way, step - 1), kind), ring_recv.at[way, step - 1, kind], dict(ring[way]))

    def pass_sem(second, way, step):
        return pass_recv.at[second, 0 if step == final else way, step - 1]

    def travels(way, step, kind):
        if step < final:
            return (step, kind) != (final - 1, 5)
        return step == final and kind < 4 and way == kind % 2

    def take(way, step, kind):
        view = slot(from_chip(way, step), kind)
        arrived(view, ring_recv.at[way, step - 1, kind])
        if travels(way, step + 1, kind):
            start(hop(way, step + 1, kind))
        if kind < 2 and step < final:
            share(way, step, kind)
        start(remote(view, pass_sem(pieces[kind][0], way, step), partner))

    def share(way, step, kind):
        chip = from_chip(way, step)
        other = xbuf.at[place(1, c, chip, pieces[kind][1], size)]
        if step == final:
            arrives = twin_recv.at[kind // 2, step - 1]
        else:
            arrives = twin_recv.at[way, step - 1] if kind < 2 else extra_recv.at[way]
        start(remote(slot(chip, kind), arrives, {"parts": 1 - here}, other))

    def take_both(step, *kinds):
        for kind in kinds:
            for way in (1, 0):
                if travels(way, step, kind):
                    take(way, step, kind)

    def across(way, step):
        first = way * shared if step == final else 0
        view = xbuf.at[place(1, c, from_chip(way, step), first, shared)]
        arrived(view, twin_recv.at[way, step - 1])
        start(remote(view, pass_sem(1, way, step), partner))

    def across_extra(way):
        view = xbuf.at[place(1, c, from_chip(way, final - 1), 3 * size, size)]
        arrived(view, extra_recv.at[way])
        start(remote(view, pass_sem(1, way, final - 1), partner))

    pltpu.make_async_copy(rows_ref, xbuf.at[pl.ds(0, p)], own_sem).wait()
    for kind in range(4):
        for way in range(2):
            start(hop(way, 1, kind))
    for second in range(2):
        start(remote(xbuf.at[place(second, c, q, 0, hp)], mine_recv, partner))
    for near in ring:
        signal(hello_sem.at[0], near)

    total[ne:nep] = jnp.zeros((nep - ne, m), F32)
    pad[ne:nep] = jnp.zeros((nep - ne, m), F32)
    orb_copy.wait()
    for j in range(m // 128):
        total[0:ne, j * 128 : (j + 1) * 128] = orb3[:, j]
    inv_copy.wait()
    pad[0:ne] = jnp.dot(inv[:, 0], total[0:ne], preferred_element_type=F32, precision=lax.Precision.HIGHEST)
    lhs[c] = pad[...].astype(BF16)
    start(remote(lhs.at[c], guest_recv, {"parts": 1 - here}, lhs.at[2 + c]))
    start(remote(lhs.at[c], pair_recv, partner))
    for chip in range(h):
        first = pl.multiple_of((chip * 2 + c) * p + here * hp, hp)
        pltpu.make_async_copy(rot_ref.at[:, pl.ds(first, hp)], rot.at[:, pl.ds(chip * hp, hp)], rot_sem).start()
    for second in range(2):
        for s in range(n):
            first = pl.multiple_of(s * p + halves[second] * hp, hp)
            pltpu.make_async_copy(
                core_ref.at[:, pl.ds(first, hp)],
                corep.at[:, pl.ds(second * side + (s % 2) * run + (s // 2) * hp, hp)],
                core_sem,
            ).start()
    lhs[4] = total[...].astype(BF16)
    dbuf[c, q] = jnp.zeros(dbuf.shape[2:], BF16)
    dtail[...] = jnp.zeros_like(dtail)
    for k in range(1, h // 2 - 1):
        pl.semaphore_wait(hello_sem.at[k - 1], 2)
        for near in ring:
            signal(hello_sem.at[k], near)
    arrived(lhs.at[1 - c], pair_recv)

    def turn(second, core, chip):
        xturn[:, columns(second, core, chip)] = xbuf[place(second, core, chip, 0, hp), :].T

    def near_block(chip, last=False):
        result = lax.dot_general(
            lhs[...].reshape(5 * nep, m), xbuf[place(0, c, chip, 0, hp), :], LAST, preferred_element_type=F32
        )
        rotated = rot[:, pl.ds(pl.multiple_of(chip * hp, hp), hp)].astype(F32)
        each = [jnp.sum(rotated * result[w * nep : w * nep + ne], axis=0, keepdims=True) for w in range(4)]
        if last:
            dlast[0, me] = jnp.concatenate(each[:2], axis=0).astype(BF16)
            dguest[...] = jnp.concatenate(each[2:], axis=0).astype(BF16)
        else:
            density = jnp.concatenate(each, axis=0).astype(BF16)
            dbuf[c, q, :, pl.ds(pl.multiple_of(chip * hp, hp), hp)] = density
        s1[:, columns(0, c, chip)] = result[4 * nep : 5 * nep]

    def block(second, core, chip):
        s1[:, columns(second, core, chip)] = lax.dot_general(
            lhs[4], xbuf[place(second, core, chip, 0, hp), :], LAST, preferred_element_type=F32
        )
        turn(second, core, chip)

    def ways(step):
        return range(2 if step < final else 1)

    def near_blocks(step):
        for way in ways(step):
            near_block(from_chip(way, step), step == final)

    def far_blocks(second, step):
        for way in ways(step):
            arrived(xbuf.at[place(second, 1 - c, from_chip(way, step), 0, hp)], pass_sem(second, way, step))
            block(second, 1 - c, from_chip(way, step))

    def turns(step):
        for way in ways(step):
            turn(0, c, from_chip(way, step))

    def second_blocks(step):
        for way in ways(step):
            block(1, c, from_chip(way, step))
        far_blocks(1, step)

    order = range(n - 1, 0, -1)

    def peer(k):
        flips = [bit for bit in range(k.bit_length()) if k >> bit & 1]
        return me + sum((1 - 2 * (me // 2**bit % 2)) * 2**bit for bit in flips)

    def send_last():
        for k in range(n - 1, -1, -1):
            target = peer(k)
            if k:
                start(remote(dlast.at[0, me], last_recv.at[0], target))
            start(remote(dguest, last_recv.at[1], {"parts": 1 - here, "chol": target}, dlast.at[1, me]))

    def gather_last():
        for guest in range(2):
            arrived(dlast.at[guest, pl.ds(0, n - 1 + guest)], last_recv.at[guest])
            for s in range(n):
                chip = s // 2
                pos = chip // 2 if chip % 2 == 0 else h - 1 - chip // 2
                first = guest * side + (s % 2) * run + chip_at(pos + final) * hp
                dtail[2 * chip : 2 * chip + 2, first : first + hp] = dlast[guest, s].astype(F32)

    block(1, c, q)
    arrived(xbuf.at[pl.ds(0, p)], mine_recv)
    block(0, 1 - c, q)
    block(1, 1 - c, q)
    take_both(1, 0, 1, 2, 3)
    pl.semaphore_wait(hello_sem.at[h // 2 - 2], 2)
    signal(ready_sem, {"chol": partner})
    arrived(lhs.at[2 + c], guest_recv)
    start(remote(lhs.at[2 + c], share_recv, partner))
    arrived(lhs.at[3 - c], share_recv)
    pltpu.make_async_copy(rot_ref.at[:, pl.ds(0, run)], rot, rot_sem).wait()
    near_block(q)
    turn(0, c, q)
    for step in range(2, final):
        take_both(step, 0, 1)
        near_blocks(step - 1)
        take_both(step, 2)
        if step < final - 1:
            far_blocks(0, step - 1)
            turns(step - 1)
        take_both(step, 3)
    near_blocks(final - 1)
    for k in range(h - 1, 0, -1):
        start(remote(dbuf.at[c, q], dens_recv, peer(2 * k)))
    for kind in (4, 5):
        for way in range(2):
            start(hop(way, 1, kind))
    pl.semaphore_wait(ready_sem, 1)
    signal(all_sem, {"parts": 1 - here})
    for way in range(2):
        across(way, 1)
    far_blocks(0, final - 2)
    turns(final - 2)
    take_both(final, 0)
    share(0, final, 0)
    take_both(final, 1, 2, 3)
    near_blocks(final)
    pl.semaphore_wait(all_sem, 1)
    send_last()
    for kind in (1, 2):
        share(0, final, kind)
    for way in range(2):
        across(way, 2)
    take_both(1, 4)
    arrived(dbuf.at[c, pl.ds(0, h - 1)], dens_recv)
    start(remote(dbuf.at[c], dpair_recv, partner))
    far_blocks(0, final - 1)
    turns(final - 1)
    take_both(1, 5)
    fields_copy.wait()
    pltpu.make_async_copy(core_ref, corep, core_sem).wait()
    arrived(dbuf.at[1 - c], dpair_recv)
    for s in range(n):
        for part in range(2):
            rows = slice(part * n + 2 * (s // 2), part * n + 2 * (s // 2) + 2)
            value = dbuf[s % 2, s // 2, 2 * part : 2 * part + 2]
            dfull[rows, (s % 2) * run : (s % 2 + 1) * run] = value.astype(F32)
    partial = lax.dot_general(dfull[...].astype(BF16), corep[:, 0:side], LAST, preferred_element_type=F32)
    fpart[...] = partial[n : 2 * n]
    start(remote(fpart, swap_recv, {"parts": 1 - here}, fother))
    share(0, final, 3)
    for way in range(2):
        share(way, final - 1, 3)
    second_blocks(1)
    take_both(2, 4)
    gather_last()
    last = lax.dot_general(dtail[...].astype(BF16), corep[...], LAST, preferred_element_type=F32)
    arrived(fother, swap_recv)
    force_bias = partial[0:n] + fother[...] + last
    fb_ref[...] = force_bias
    shifted = (fields[...] - force_bias).astype(BF16)
    potentials = []
    for a in range(2):
        parts = [
            jnp.dot(shifted, corep[:, first : first + run], preferred_element_type=F32)
            for first in (a * side, a * side + run)
        ]
        for w in range(n):
            pbuf[a, w] = jnp.concatenate([part[w : w + 1] for part in parts], axis=0).astype(BF16)
        for k in order:
            target = peer(k)
            copy = remote(pbuf.at[a, target], pot_recv.at[a], target, rbuf.at[a, k - 1], pot_send)
            copy.start()
            potentials.append(copy)
    take_both(2, 5)
    for way in range(2):
        across(way, final - 1)
    second_blocks(2)
    far_blocks(0, final)
    turns(final)
    for way in range(2):
        across(way, final)
    take_both(final - 1, 4)
    second_blocks(final)
    for way in range(2):
        across_extra(way)
    second_blocks(final - 1)
    for copy in sent:
        copy.wait_send()

    wide = 512
    for a in range(2):
        half = slice(a * side, (a + 1) * side)
        summed = pbuf[a, me].astype(F32)
        arrived(rbuf.at[a], pot_recv.at[a])
        for k in order:
            summed = summed + rbuf[a, k - 1].astype(F32)
        for core in range(2):
            where = slice(a * side + core * run, a * side + (core + 1) * run)
            pot[:, where] = summed[core : core + 1]
            sc[:, where] = (s1[:, where] * summed[core : core + 1]).astype(BF16)
        for j in range(m // wide):
            where = slice(j * wide, (j + 1) * wide)
            result = jnp.dot(sc[:, half], xbuf[half, where], preferred_element_type=F32)
            if a == 0:
                early[:, where] = result
            else:
                result = early[:, where] + result
                total[:, where] += result
                tbf[:, where] = result.astype(BF16)
    for order in range(2, TAYLOR + 1):
        for a in range(2):
            half = slice(a * side, (a + 1) * side)
            result = jnp.dot(tbf[...], xturn[:, half], preferred_element_type=F32)
            sc[:, half] = (result * (pot[:, half] / order)).astype(BF16)
        for j in range(m // wide):
            where = slice(j * wide, (j + 1) * wide)
            result = jnp.dot(sc[...], xbuf[:, where], preferred_element_type=F32)
            if order < TAYLOR:
                total[:, where] += result
                tbf[:, where] = result.astype(BF16)
            else:
                for i in range(wide // 128):
                    at = slice(j * wide + i * 128, j * wide + (i + 1) * 128)
                    out_ref[:, j * (wide // 128) + i] = total[0:ne, at] + result[0:ne, i * 128 : (i + 1) * 128]
    for copy in potentials:
        copy.wait_send()


def fused(orbitals, intersection_inv, factor_rows, factor_rotated, factor_core, fields, n):
    h = n // 2
    p, m = factor_rows.shape
    ne, points = factor_rotated.shape
    nep = -(-ne // 16) * 16
    hp = p // 2
    run, side = h * hp, n * hp
    vmem = pl.BlockSpec(memory_space=pltpu.VMEM)
    hbm = pl.BlockSpec(memory_space=pl.ANY)
    dma = pltpu.SemaphoreType.DMA
    propagated, force_bias = pl.pallas_call(
        functools.partial(kernel, n),
        out_shape=(pltpu.VMEM((ne, m // 128, 128), F32), pltpu.VMEM(fields.shape, F32)),
        in_specs=[hbm] * 6,
        out_specs=(vmem, vmem),
        scratch_shapes=[
            pltpu.VMEM((points, m), BF16),
            pltpu.VMEM((m, points), BF16),
            pltpu.VMEM((ne, m // 128, 128), F32),
            pltpu.VMEM((ne, 1, ne), F32),
            pltpu.VMEM(fields.shape, F32),
            pltpu.VMEM((5, nep, m), BF16),
            pltpu.VMEM((nep, m), F32),
            pltpu.VMEM((ne, run), BF16),
            pltpu.VMEM(factor_core.shape, BF16),
            pltpu.VMEM((nep, points), F32),
            pltpu.VMEM((nep, points), BF16),
            pltpu.VMEM((2, h, 4, run), BF16),
            pltpu.VMEM((2, n, 2, hp), BF16),
            pltpu.VMEM((2, hp), BF16),
            pltpu.VMEM((2 * n, side), F32),
            pltpu.VMEM((n, points), F32),
            pltpu.VMEM(fields.shape, F32),
            pltpu.VMEM(fields.shape, F32),
            pltpu.VMEM((2, n, 2, run), BF16),
            pltpu.VMEM((2, n - 1, 2, run), BF16),
            pltpu.VMEM((1, points), F32),
            pltpu.VMEM((nep, m), BF16),
            pltpu.VMEM((nep, m), F32),
            pltpu.VMEM((nep, m), F32),
            *[dma(())] * 15,
            pltpu.SemaphoreType.REGULAR,
            pltpu.SemaphoreType.REGULAR,
            dma((2, h // 2, 6)),
            dma((2, h // 2)),
            dma((2,)),
            dma((2, 2, h // 2)),
            dma((2,)),
            dma((2,)),
            pltpu.SemaphoreType.REGULAR((h // 2 - 1,)),
        ],
        compiler_params=pltpu.CompilerParams(
            collective_id=0, has_side_effects=True, vmem_limit_bytes=60 * 1024 * 1024
        ),
    )(
        orbitals.reshape(ne, m // 128, 128), intersection_inv.reshape(ne, 1, ne),
        factor_rows, factor_rotated, factor_core, fields,
    )
    pieces = 4
    propagated, force_bias = pl.pallas_call(
        functools.partial(write_out, pieces),
        out_shape=(
            jax.ShapeDtypeStruct(propagated.shape, F32),
            jax.ShapeDtypeStruct(fields.shape, F32),
        ),
        in_specs=[vmem] * 2,
        out_specs=(hbm, hbm),
        scratch_shapes=[dma((pieces + 1,))],
    )(*(pltpu.with_memory_space_constraint(value, pltpu.VMEM) for value in (propagated, force_bias)))
    return propagated.reshape(orbitals.shape), force_bias


def write_out(pieces, propagated, force_bias, out_ref, fb_ref, sem):
    size = propagated.shape[0] // pieces
    copies = [pltpu.make_async_copy(force_bias, fb_ref, sem.at[pieces])]
    for i in range(pieces):
        where = pl.ds(i * size, size)
        copies.append(pltpu.make_async_copy(propagated.at[where], out_ref.at[where], sem.at[i]))
    for copy in copies:
        copy.start()
    for copy in copies:
        copy.wait()


def density_one(half_green, all_rows, factor_rotated):
    projected = lax.dot_general(half_green, all_rows, LAST, preferred_element_type=F32)
    return jnp.sum(factor_rotated.astype(F32) * projected, axis=0).astype(BF16)


def propagate_one(orbital, potential, all_rows):
    total = orbital
    term = orbital
    for order in range(1, TAYLOR + 1):
        summed = lax.dot_general(term.astype(BF16), all_rows, LAST, preferred_element_type=F32)
        scaled = (summed * potential[None, :] / order).astype(BF16)
        term = jnp.dot(scaled, all_rows, preferred_element_type=F32)
        total = total + term
    return total


def plain(orbitals, intersection_inv, factor_rows, factor_rotated, factor_core, fields):
    walker_count = orbitals.shape[0]
    half_green = jnp.einsum(
        "wij,wjm->wim", intersection_inv, orbitals, precision=lax.Precision.HIGHEST
    ).astype(BF16)
    all_rows = lax.all_gather(factor_rows, "chol", axis=0, tiled=True)
    own_density = lax.map(lambda item: density_one(item, all_rows, factor_rotated), half_green)
    density = lax.all_gather(own_density, "chol", axis=0, tiled=True)
    force_bias = lax.dot_general(density, factor_core, LAST, preferred_element_type=F32)
    shifted = (fields - force_bias).astype(BF16)
    partial_sum = jnp.dot(shifted, factor_core, preferred_element_type=F32)
    summed_all = lax.psum(partial_sum, "chol")
    potential = lax.dynamic_slice_in_dim(
        summed_all, lax.axis_index("chol") * walker_count, walker_count, 0
    )
    propagated = lax.map(lambda pair: propagate_one(pair[0], pair[1], all_rows), (orbitals, potential))
    return (propagated, force_bias)


def solution(mesh):
    n = mesh.shape["chol"]

    def on_device(orbitals, intersection_inv, factor_rows, factor_rotated, factor_core, fields):
        args = (orbitals, intersection_inv, factor_rows, factor_rotated, factor_core, fields)
        rows, m = factor_rows.shape
        if orbitals.shape[0] == 1 and n == 16 and rows % 256 == 0 and mesh.shape["parts"] == 2 and m % 512 == 0:
            return fused(*args, n)
        return plain(*args)

    in_specs = (
        P(("parts", "chol"), None, None),
        P(("parts", "chol"), None, None),
        P("chol", None),
        P(),
        P("chol", None),
        P("parts", "chol"),
    )
    out_specs = (P(("parts", "chol"), None, None), P("parts", "chol"))
    return jax.shard_map(
        on_device, mesh=mesh, in_specs=in_specs, out_specs=out_specs, check_vma=False
    )
```

```python
import functools

import jax
import jax.numpy as jnp
from jax import lax
from jax.experimental import pallas as pl
from jax.experimental.pallas import tpu as pltpu
from jax.sharding import PartitionSpec as P

TAYLOR = 4
F32, BF16 = jnp.float32, jnp.bfloat16
LAST = (((1,), (1,)), ((), ()))


def kernel(
    n, orb_ref, inv_ref, rows_ref, rot_ref, core_ref, fields_ref, out_ref, fb_ref,
    xbuf, xturn, orb3, inv, fields, lhs, pad, rot, corep, s1, sc, dbuf, dlast, dguest, dfull, dtail, fpart, fother, pbuf, rbuf, pot,
    tbf, total, early,
    orb_sem, inv_sem, fields_sem, own_sem, rot_sem, core_sem, send_sem, pair_recv, guest_recv, share_recv, mine_recv,
    dens_recv, dpair_recv, swap_recv, pot_send, ready_sem, all_sem, ring_recv, twin_recv, extra_recv, pass_recv, last_recv, pot_recv, hello_sem,
):
    h = n // 2
    p, m = rows_ref.shape
    ne = orb_ref.shape[0]
    nep = pad.shape[0]
    hp = p // 2
    run = h * hp
    side = n * hp
    shared = hp // 2
    size = shared // 2
    final = h // 2
    here = lax.axis_index("parts")
    me = lax.axis_index("chol")
    q, c = me // 2, me % 2
    partner = q * 2 + (1 - c)
    r = (1 - q % 2) * (q // 2) + (q % 2) * (h - 1 - q // 2)
    halves = (here, 1 - here)

    pieces = ((0, 0), (0, size), (0, 2 * size), (0, 3 * size), (1, 2 * size), (1, 3 * size))

    def chip_at(pos):
        pos = (pos + 2 * h) % h
        s = pos // (h // 2)
        return (1 - s) * 2 * pos + s * (2 * (h - 1 - pos) + 1)

    def signal(sem, device):
        pl.semaphore_signal(sem, inc=1, device_id=device, device_id_type=pl.DeviceIdType.MESH)

    barrier = pltpu.get_barrier_semaphore()
    ring = ({"chol": chip_at(r + 1) * 2 + c}, {"chol": chip_at(r - 1) * 2 + c})
    for near in ({"chol": partner}, *ring, {"parts": 1 - here}):
        signal(barrier, near)

    def place(second, core, chip, first, size):
        return pl.ds(pl.multiple_of(second * side + core * run + chip * hp + first, 16), size)

    def columns(second, core, chip):
        return pl.ds(pl.multiple_of(second * side + core * run + chip * hp, hp), hp)

    for second in range(2):
        pltpu.make_async_copy(
            rows_ref.at[pl.ds(pl.multiple_of(halves[second] * hp, hp), hp)], xbuf.at[place(second, c, q, 0, hp)], own_sem
        ).start()
    orb_copy = pltpu.make_async_copy(orb_ref, orb3, orb_sem)
    orb_copy.start()
    inv_copy = pltpu.make_async_copy(inv_ref, inv, inv_sem)
    inv_copy.start()
    fields_copy = pltpu.make_async_copy(fields_ref, fields, fields_sem)
    fields_copy.start()

    pl.semaphore_wait(barrier, 4)
    sent = []

    def remote(view, recv, target, dst=None, send=send_sem):
        return pltpu.make_async_remote_copy(
            src_ref=view, dst_ref=view if dst is None else dst, send_sem=send, recv_sem=recv,
            device_id=target if isinstance(target, dict) else {"chol": target}, device_id_type=pl.DeviceIdType.MESH,
        )

    def arrived(view, recv):
        remote(view, recv, partner).wait_recv()

    def start(copy):
        copy.start()
        sent.append(copy)

    def from_chip(way, step):
        return chip_at(r - (1 - 2 * way) * step)

    def slot(chip, kind):
        second, first = pieces[kind]
        return xbuf.at[place(second, c, chip, first, size)]

    def hop(way, step, kind):
        return remote(slot(from_chip(way, step - 1), kind), ring_recv.at[way, step - 1, kind], dict(ring[way]))

    def pass_sem(second, way, step):
        return pass_recv.at[second, 0 if step == final else way, step - 1]

    def travels(way, step, kind):
        if step < final:
            return (step, kind) != (final - 1, 5)
        return step == final and kind < 4 and way == kind % 2

    def take(way, step, kind):
        view = slot(from_chip(way, step), kind)
        arrived(view, ring_recv.at[way, step - 1, kind])
        if travels(way, step + 1, kind):
            start(hop(way, step + 1, kind))
        if kind < 2 and step < final:
            share(way, step, kind)
        start(remote(view, pass_sem(pieces[kind][0], way, step), partner))

    def share(way, step, kind):
        chip = from_chip(way, step)
        other = xbuf.at[place(1, c, chip, pieces[kind][1], size)]
        if step == final:
            arrives = twin_recv.at[kind // 2, step - 1]
        else:
            arrives = twin_recv.at[way, step - 1] if kind < 2 else extra_recv.at[way]
        start(remote(slot(chip, kind), arrives, {"parts": 1 - here}, other))

    def take_both(step, *kinds):
        for kind in kinds:
            for way in (1, 0):
                if travels(way, step, kind):
                    take(way, step, kind)

    def across(way, step):
        first = way * shared if step == final else 0
        view = xbuf.at[place(1, c, from_chip(way, step), first, shared)]
        arrived(view, twin_recv.at[way, step - 1])
        start(remote(view, pass_sem(1, way, step), partner))

    def across_extra(way):
        view = xbuf.at[place(1, c, from_chip(way, final - 1), 3 * size, size)]
        arrived(view, extra_recv.at[way])
        start(remote(view, pass_sem(1, way, final - 1), partner))

    pltpu.make_async_copy(rows_ref, xbuf.at[pl.ds(0, p)], own_sem).wait()
    for kind in range(4):
        for way in range(2):
            start(hop(way, 1, kind))
    for second in range(2):
        start(remote(xbuf.at[place(second, c, q, 0, hp)], mine_recv, partner))
    for near in ring:
        signal(hello_sem.at[0], near)

    total[ne:nep] = jnp.zeros((nep - ne, m), F32)
    pad[ne:nep] = jnp.zeros((nep - ne, m), F32)
    orb_copy.wait()
    for j in range(m // 128):
        total[0:ne, j * 128 : (j + 1) * 128] = orb3[:, j]
    inv_copy.wait()
    pad[0:ne] = jnp.dot(inv[:, 0], total[0:ne], preferred_element_type=F32, precision=lax.Precision.HIGHEST)
    lhs[c] = pad[...].astype(BF16)
    start(remote(lhs.at[c], guest_recv, {"parts": 1 - here}, lhs.at[2 + c]))
    start(remote(lhs.at[c], pair_recv, partner))
    for chip in range(h):
        first = pl.multiple_of((chip * 2 + c) * p + here * hp, hp)
        pltpu.make_async_copy(rot_ref.at[:, pl.ds(first, hp)], rot.at[:, pl.ds(chip * hp, hp)], rot_sem).start()
    for second in range(2):
        for s in range(n):
            first = pl.multiple_of(s * p + halves[second] * hp, hp)
            pltpu.make_async_copy(
                core_ref.at[:, pl.ds(first, hp)],
                corep.at[:, pl.ds(second * side + (s % 2) * run + (s // 2) * hp, hp)],
                core_sem,
            ).start()
    lhs[4] = total[...].astype(BF16)
    dbuf[c, q] = jnp.zeros(dbuf.shape[2:], BF16)
    dtail[...] = jnp.zeros_like(dtail)
    for k in range(1, h // 2 - 1):
        pl.semaphore_wait(hello_sem.at[k - 1], 2)
        for near in ring:
            signal(hello_sem.at[k], near)
    arrived(lhs.at[1 - c], pair_recv)

    def turn(second, core, chip):
        xturn[:, columns(second, core, chip)] = xbuf[place(second, core, chip, 0, hp), :].T

    def near_block(chip, last=False):
        count = 4 if last else 5
        result = lax.dot_general(
            lhs[0:count].reshape(count * nep, m), xbuf[place(0, c, chip, 0, hp), :], LAST, preferred_element_type=F32
        )
        rotated = rot[:, pl.ds(pl.multiple_of(chip * hp, hp), hp)].astype(F32)
        each = [jnp.sum(rotated * result[w * nep : w * nep + ne], axis=0, keepdims=True) for w in range(4)]
        if last:
            dlast[0, me] = jnp.concatenate(each[:2], axis=0).astype(BF16)
            dguest[...] = jnp.concatenate(each[2:], axis=0).astype(BF16)
        else:
            density = jnp.concatenate(each, axis=0).astype(BF16)
            dbuf[c, q, :, pl.ds(pl.multiple_of(chip * hp, hp), hp)] = density
        if not last:
            s1[:, columns(0, c, chip)] = result[4 * nep : 5 * nep]

    def block(second, core, chip):
        s1[:, columns(second, core, chip)] = lax.dot_general(
            lhs[4], xbuf[place(second, core, chip, 0, hp), :], LAST, preferred_element_type=F32
        )
        turn(second, core, chip)

    def ways(step):
        return range(2 if step < final else 1)

    def near_blocks(step):
        for way in ways(step):
            near_block(from_chip(way, step), step == final)

    def far_blocks(second, step):
        for way in ways(step):
            arrived(xbuf.at[place(second, 1 - c, from_chip(way, step), 0, hp)], pass_sem(second, way, step))
            block(second, 1 - c, from_chip(way, step))

    def turns(step):
        for way in ways(step):
            turn(0, c, from_chip(way, step))

    def second_blocks(step):
        for way in ways(step):
            block(1, c, from_chip(way, step))
        far_blocks(1, step)

    order = range(n - 1, 0, -1)

    def peer(k):
        flips = [bit for bit in range(k.bit_length()) if k >> bit & 1]
        return me + sum((1 - 2 * (me // 2**bit % 2)) * 2**bit for bit in flips)

    def send_last():
        for k in range(n - 1, -1, -1):
            target = peer(k)
            if k:
                start(remote(dlast.at[0, me], last_recv.at[0], target))
            start(remote(dguest, last_recv.at[1], {"parts": 1 - here, "chol": target}, dlast.at[1, me]))

    def gather_last():
        for guest in range(2):
            arrived(dlast.at[guest, pl.ds(0, n - 1 + guest)], last_recv.at[guest])
            for s in range(n):
                chip = s // 2
                pos = chip // 2 if chip % 2 == 0 else h - 1 - chip // 2
                first = guest * side + (s % 2) * run + chip_at(pos + final) * hp
                dtail[2 * chip : 2 * chip + 2, first : first + hp] = dlast[guest, s].astype(F32)

    block(1, c, q)
    arrived(xbuf.at[pl.ds(0, p)], mine_recv)
    block(0, 1 - c, q)
    block(1, 1 - c, q)
    take_both(1, 0, 1, 2, 3)
    pl.semaphore_wait(hello_sem.at[h // 2 - 2], 2)
    signal(ready_sem, {"chol": partner})
    arrived(lhs.at[2 + c], guest_recv)
    start(remote(lhs.at[2 + c], share_recv, partner))
    arrived(lhs.at[3 - c], share_recv)
    pltpu.make_async_copy(rot_ref.at[:, pl.ds(0, run)], rot, rot_sem).wait()
    near_block(q)
    turn(0, c, q)
    for step in range(2, final):
        take_both(step, 0, 1)
        near_blocks(step - 1)
        take_both(step, 2)
        if step < final - 1:
            far_blocks(0, step - 1)
            turns(step - 1)
        take_both(step, 3)
    near_blocks(final - 1)
    for k in range(h - 1, 0, -1):
        start(remote(dbuf.at[c, q], dens_recv, peer(2 * k)))
    for kind in (4, 5):
        for way in range(2):
            start(hop(way, 1, kind))
    pl.semaphore_wait(ready_sem, 1)
    signal(all_sem, {"parts": 1 - here})
    for way in range(2):
        across(way, 1)
    far_blocks(0, final - 2)
    turns(final - 2)
    take_both(final, 0)
    share(0, final, 0)
    take_both(final, 1, 2, 3)
    near_blocks(final)
    pl.semaphore_wait(all_sem, 1)
    send_last()
    for kind in (1, 2):
        share(0, final, kind)
    for way in range(2):
        across(way, 2)
    take_both(1, 4)
    arrived(dbuf.at[c, pl.ds(0, h - 1)], dens_recv)
    start(remote(dbuf.at[c], dpair_recv, partner))
    far_blocks(0, final - 1)
    turns(final - 1)
    take_both(1, 5)
    fields_copy.wait()
    pltpu.make_async_copy(core_ref, corep, core_sem).wait()
    arrived(dbuf.at[1 - c], dpair_recv)
    for s in range(n):
        for part in range(2):
            rows = slice(part * n + 2 * (s // 2), part * n + 2 * (s // 2) + 2)
            value = dbuf[s % 2, s // 2, 2 * part : 2 * part + 2]
            dfull[rows, (s % 2) * run : (s % 2 + 1) * run] = value.astype(F32)
    partial = lax.dot_general(dfull[...].astype(BF16), corep[:, 0:side], LAST, preferred_element_type=F32)
    fpart[...] = partial[n : 2 * n]
    start(remote(fpart, swap_recv, {"parts": 1 - here}, fother))
    share(0, final, 3)
    for way in range(2):
        share(way, final - 1, 3)
    second_blocks(1)
    take_both(2, 4)
    gather_last()
    last = lax.dot_general(dtail[...].astype(BF16), corep[...], LAST, preferred_element_type=F32)
    arrived(fother, swap_recv)
    force_bias = partial[0:n] + fother[...] + last
    fb_ref[...] = force_bias
    shifted = (fields[...] - force_bias).astype(BF16)
    potentials = []
    for a in range(2):
        parts = [
            jnp.dot(shifted, corep[:, first : first + run], preferred_element_type=F32)
            for first in (a * side, a * side + run)
        ]
        for w in range(n):
            pbuf[a, w] = jnp.concatenate([part[w : w + 1] for part in parts], axis=0).astype(BF16)
        for k in order:
            target = peer(k)
            copy = remote(pbuf.at[a, target], pot_recv.at[a], target, rbuf.at[a, k - 1], pot_send)
            copy.start()
            potentials.append(copy)
    take_both(2, 5)
    for way in range(2):
        across(way, final - 1)
    second_blocks(2)
    far_blocks(0, final)
    block(0, c, from_chip(0, final))
    for way in range(2):
        across(way, final)
    take_both(final - 1, 4)
    second_blocks(final)
    for way in range(2):
        across_extra(way)
    second_blocks(final - 1)
    for copy in sent:
        copy.wait_send()

    wide = 512
    for a in range(2):
        half = slice(a * side, (a + 1) * side)
        summed = pbuf[a, me].astype(F32)
        arrived(rbuf.at[a], pot_recv.at[a])
        for k in order:
            summed = summed + rbuf[a, k - 1].astype(F32)
        for core in range(2):
            where = slice(a * side + core * run, a * side + (core + 1) * run)
            pot[:, where] = summed[core : core + 1]
            sc[:, where] = (s1[:, where] * summed[core : core + 1]).astype(BF16)
        for j in range(m // wide):
            where = slice(j * wide, (j + 1) * wide)
            result = jnp.dot(sc[:, half], xbuf[half, where], preferred_element_type=F32)
            if a == 0:
                early[:, where] = result
            else:
                result = early[:, where] + result
                total[:, where] += result
                tbf[:, where] = result.astype(BF16)
    for order in range(2, TAYLOR + 1):
        for a in range(2):
            half = slice(a * side, (a + 1) * side)
            result = jnp.dot(tbf[...], xturn[:, half], preferred_element_type=F32)
            sc[:, half] = (result * (pot[:, half] / order)).astype(BF16)
        for j in range(m // wide):
            where = slice(j * wide, (j + 1) * wide)
            result = jnp.dot(sc[...], xbuf[:, where], preferred_element_type=F32)
            if order < TAYLOR:
                total[:, where] += result
                tbf[:, where] = result.astype(BF16)
            else:
                for i in range(wide // 128):
                    at = slice(j * wide + i * 128, j * wide + (i + 1) * 128)
                    out_ref[:, j * (wide // 128) + i] = total[0:ne, at] + result[0:ne, i * 128 : (i + 1) * 128]
    for copy in potentials:
        copy.wait_send()


def fused(orbitals, intersection_inv, factor_rows, factor_rotated, factor_core, fields, n):
    h = n // 2
    p, m = factor_rows.shape
    ne, points = factor_rotated.shape
    nep = -(-ne // 16) * 16
    hp = p // 2
    run, side = h * hp, n * hp
    vmem = pl.BlockSpec(memory_space=pltpu.VMEM)
    hbm = pl.BlockSpec(memory_space=pl.ANY)
    dma = pltpu.SemaphoreType.DMA
    propagated, force_bias = pl.pallas_call(
        functools.partial(kernel, n),
        out_shape=(pltpu.VMEM((ne, m // 128, 128), F32), pltpu.VMEM(fields.shape, F32)),
        in_specs=[hbm] * 6,
        out_specs=(vmem, vmem),
        scratch_shapes=[
            pltpu.VMEM((points, m), BF16),
            pltpu.VMEM((m, points), BF16),
            pltpu.VMEM((ne, m // 128, 128), F32),
            pltpu.VMEM((ne, 1, ne), F32),
            pltpu.VMEM(fields.shape, F32),
            pltpu.VMEM((5, nep, m), BF16),
            pltpu.VMEM((nep, m), F32),
            pltpu.VMEM((ne, run), BF16),
            pltpu.VMEM(factor_core.shape, BF16),
            pltpu.VMEM((nep, points), F32),
            pltpu.VMEM((nep, points), BF16),
            pltpu.VMEM((2, h, 4, run), BF16),
            pltpu.VMEM((2, n, 2, hp), BF16),
            pltpu.VMEM((2, hp), BF16),
            pltpu.VMEM((2 * n, side), F32),
            pltpu.VMEM((n, points), F32),
            pltpu.VMEM(fields.shape, F32),
            pltpu.VMEM(fields.shape, F32),
            pltpu.VMEM((2, n, 2, run), BF16),
            pltpu.VMEM((2, n - 1, 2, run), BF16),
            pltpu.VMEM((1, points), F32),
            pltpu.VMEM((nep, m), BF16),
            pltpu.VMEM((nep, m), F32),
            pltpu.VMEM((nep, m), F32),
            *[dma(())] * 15,
            pltpu.SemaphoreType.REGULAR,
            pltpu.SemaphoreType.REGULAR,
            dma((2, h // 2, 6)),
            dma((2, h // 2)),
            dma((2,)),
            dma((2, 2, h // 2)),
            dma((2,)),
            dma((2,)),
            pltpu.SemaphoreType.REGULAR((h // 2 - 1,)),
        ],
        compiler_params=pltpu.CompilerParams(
            collective_id=0, has_side_effects=True, vmem_limit_bytes=60 * 1024 * 1024
        ),
    )(
        orbitals.reshape(ne, m // 128, 128), intersection_inv.reshape(ne, 1, ne),
        factor_rows, factor_rotated, factor_core, fields,
    )
    pieces = 4
    propagated, force_bias = pl.pallas_call(
        functools.partial(write_out, pieces),
        out_shape=(
            jax.ShapeDtypeStruct(propagated.shape, F32),
            jax.ShapeDtypeStruct(fields.shape, F32),
        ),
        in_specs=[vmem] * 2,
        out_specs=(hbm, hbm),
        scratch_shapes=[dma((pieces + 1,))],
    )(*(pltpu.with_memory_space_constraint(value, pltpu.VMEM) for value in (propagated, force_bias)))
    return propagated.reshape(orbitals.shape), force_bias


def write_out(pieces, propagated, force_bias, out_ref, fb_ref, sem):
    size = propagated.shape[0] // pieces
    copies = [pltpu.make_async_copy(force_bias, fb_ref, sem.at[pieces])]
    for i in range(pieces):
        where = pl.ds(i * size, size)
        copies.append(pltpu.make_async_copy(propagated.at[where], out_ref.at[where], sem.at[i]))
    for copy in copies:
        copy.start()
    for copy in copies:
        copy.wait()


def density_one(half_green, all_rows, factor_rotated):
    projected = lax.dot_general(half_green, all_rows, LAST, preferred_element_type=F32)
    return jnp.sum(factor_rotated.astype(F32) * projected, axis=0).astype(BF16)


def propagate_one(orbital, potential, all_rows):
    total = orbital
    term = orbital
    for order in range(1, TAYLOR + 1):
        summed = lax.dot_general(term.astype(BF16), all_rows, LAST, preferred_element_type=F32)
        scaled = (summed * potential[None, :] / order).astype(BF16)
        term = jnp.dot(scaled, all_rows, preferred_element_type=F32)
        total = total + term
    return total


def plain(orbitals, intersection_inv, factor_rows, factor_rotated, factor_core, fields):
    walker_count = orbitals.shape[0]
    half_green = jnp.einsum(
        "wij,wjm->wim", intersection_inv, orbitals, precision=lax.Precision.HIGHEST
    ).astype(BF16)
    all_rows = lax.all_gather(factor_rows, "chol", axis=0, tiled=True)
    own_density = lax.map(lambda item: density_one(item, all_rows, factor_rotated), half_green)
    density = lax.all_gather(own_density, "chol", axis=0, tiled=True)
    force_bias = lax.dot_general(density, factor_core, LAST, preferred_element_type=F32)
    shifted = (fields - force_bias).astype(BF16)
    partial_sum = jnp.dot(shifted, factor_core, preferred_element_type=F32)
    summed_all = lax.psum(partial_sum, "chol")
    potential = lax.dynamic_slice_in_dim(
        summed_all, lax.axis_index("chol") * walker_count, walker_count, 0
    )
    propagated = lax.map(lambda pair: propagate_one(pair[0], pair[1], all_rows), (orbitals, potential))
    return (propagated, force_bias)


def solution(mesh):
    n = mesh.shape["chol"]

    def on_device(orbitals, intersection_inv, factor_rows, factor_rotated, factor_core, fields):
        args = (orbitals, intersection_inv, factor_rows, factor_rotated, factor_core, fields)
        rows, m = factor_rows.shape
        if orbitals.shape[0] == 1 and n == 16 and rows % 256 == 0 and mesh.shape["parts"] == 2 and m % 512 == 0:
            return fused(*args, n)
        return plain(*args)

    in_specs = (
        P(("parts", "chol"), None, None),
        P(("parts", "chol"), None, None),
        P("chol", None),
        P(),
        P("chol", None),
        P("parts", "chol"),
    )
    out_specs = (P(("parts", "chol"), None, None), P("parts", "chol"))
    return jax.shard_map(
        on_device, mesh=mesh, in_specs=in_specs, out_specs=out_specs, check_vma=False
    )
```
